256 devices in a mesh: seq: 16 (over y, z_lo, core), head: 16 (over z_hi, x).
Axes of the slice: x: 4, y: 4, z: 8 (z_hi: 4, z_lo: 2; z = z_hi * 2 + z_lo), core: 2. Of those that a mesh axis runs over, the one named last changes fastest.
Arguments:
- query_latent: bfloat16 [4096, 128, 576], P('seq', 'head'), may hold values from -6 to 6
- key_latent: bfloat16 [2048, 576], P('seq'), may hold values from -6 to 6
- normalizer: float32 [4096, 128], P('seq', 'head'), may hold values from 7 to 9
- index_query: bfloat16 [4096, 64, 128], P('seq', 'head'), may hold values from -20 to 20
- index_key: bfloat16 [2048, 128], P('seq'), may hold values from -6.5 to 6.5
- index_weight: float32 [4096, 64], P('seq', 'head'), may hold values from 0.05 to 0.5
- kept: int32 [32, 16], P('seq'), may hold values from 0 to 1, as said below
Outputs:
- index_query_grad: bfloat16 [4096, 64, 128], P('seq', 'head')
- index_key_grad: float32 [2048, 128], P('seq')
The draws below stay inside these ranges and needn't reach their ends.
Inputs may be any that keep to these rules, and one draw needn't show every extreme that they name: `kept`: every query tile keeps the key tile whose position matches its own block of 256 queries.
All inputs are finite; a program needn't handle non-finite values.
Results may differ from the reference program's by a relative error of at most 0.009.
Values may be sent and summed in bfloat16 or wider, within the bound.
No kernel may reach another device: no remote copies, remote signals or barrier semaphores. Data moves between devices by JAX's collectives and lax.ppermute only.
A program may use at most 64 MiB of HBM per device.

```python
import math
import jax
import jax.numpy as jnp
from jax import lax

H = 128
LATENT = 512
ROPE = 64
IH = 64
ID = 128
TILE = 128
Q_DEV = 256
QUERIES = 4096
KEYS = 2048
N_SEQ = 16


def base_keys(key):
    values = jax.random.normal(jax.random.fold_in(key, 7), (KEYS, ID), jnp.float32)
    return jnp.clip(values, -6.0, 6.0)


def draw_index_key(key, part):
    values = base_keys(key)
    return values.astype(jnp.bfloat16)


def draw_index_query(key, part):
    values = jax.random.normal(jax.random.fold_in(key, 11), (QUERIES, IH, ID), jnp.float32)
    values = jnp.clip(values, -6.0, 6.0)
    return values.astype(jnp.bfloat16)


def draw_kept(key, part):
    tiles = QUERIES // TILE
    rate = jax.random.randint(jax.random.fold_in(key, 3), (tiles, 1), 55, 101)
    roll = jax.random.randint(jax.random.fold_in(key, 5), (tiles, N_SEQ), 0, 100)
    own_tile = jnp.arange(tiles)[:, None] // (Q_DEV // TILE) == jnp.arange(N_SEQ)[None, :]
    return jnp.where(own_tile | (roll < rate), 1, 0).astype(jnp.int32)


def block_levels(own_key, shape, shards, smallest, largest):
    level = 1.0
    for axis_at, blocks in shards:
        steps = jax.random.uniform(jax.random.fold_in(jax.random.fold_in(own_key, 6), axis_at), (blocks,), jnp.float32, smallest / len(shards), largest / len(shards))
        level = level * jnp.repeat(jnp.exp(steps), shape[axis_at] // blocks).reshape((-1,) + (1,) * (len(shape) - 1 - axis_at))
    return level


def centred(rng, shape, scale, bound, pieces=(), dtype=jnp.bfloat16):
    level = block_levels(rng, shape, pieces, -0.22, 0.18) if pieces else 1.0
    values = jax.random.normal(rng, shape, jnp.float32) * scale * level
    return jnp.minimum(jnp.maximum(values, -bound), bound).astype(dtype)


def setup_inputs(seed: int = 0) -> dict:
    key_list = jax.random.split(jax.random.key(seed), 8)
    return {
        "query_latent": centred(key_list[0], (QUERIES, H, LATENT + ROPE), 1.0, 6.0, ((0, 16), (1, 16))),
        "key_latent": centred(key_list[1], (KEYS, LATENT + ROPE), 1.0, 6.0, ((0, 16),)),
        "normalizer": jnp.clip(7.0 + 2.0 * jax.random.uniform(key_list[2], (QUERIES, H), jnp.float32) ** block_levels(key_list[2], (QUERIES, H), ((0, 16), (1, 16)), -0.2, 0.2), 7.0, 9.0),
        "index_query": draw_index_query(jax.random.fold_in(key_list[7], 71), 0),
        "index_key": draw_index_key(jax.random.fold_in(key_list[7], 71), 0),
        "index_weight": jnp.clip(jnp.exp(math.log(0.5) - 2.3025851 * jax.random.uniform(key_list[5], (QUERIES, IH), jnp.float32) ** block_levels(key_list[5], (QUERIES, IH), ((0, 16), (1, 16)), -0.2, 0.2)), 0.05, 0.5),
        "kept": draw_kept(jax.random.fold_in(key_list[7], 71), 0),
    }


attn_scale = 192.0 ** -0.5


def reference(query_latent, key_latent, normalizer, index_query, index_key, index_weight, kept):
    tiles = QUERIES // TILE
    width = LATENT + ROPE
    index_scale = ID ** -0.5
    allow_cols = jnp.repeat(kept, TILE, axis=1) > 0
    query_tiles = query_latent.reshape(tiles, TILE, H, width)
    norm_tiles = normalizer.reshape(tiles, TILE, H)
    iquery_tiles = index_query.reshape(tiles, TILE, IH, ID)
    weight_tiles = index_weight.reshape(tiles, TILE, IH)
    keys_f = index_key.astype(jnp.float32)

    def one_tile(carry, parts):
        query, lse, iquery, weight, keep = parts
        scores = jnp.dot(query.reshape(TILE * H, width), key_latent.T, preferred_element_type=jnp.float32) * attn_scale
        prob = jnp.exp(scores.reshape(TILE, H, KEYS) - lse[:, :, None])
        head_sum = jnp.where(keep[None, :], jnp.sum(prob, axis=1), 0.0)
        target = head_sum / jnp.sum(head_sum, axis=1, keepdims=True)
        z_val = jnp.einsum('tjd,sd->tjs', iquery.astype(jnp.float32), keys_f) * index_scale
        logit = jnp.sum(weight[:, :, None] * jnp.maximum(z_val, 0.0), axis=1)
        top = jnp.max(jnp.where(keep[None, :], logit, -jnp.inf), axis=1, keepdims=True)
        expo = jnp.where(keep[None, :], jnp.exp(jnp.where(keep[None, :], logit, top) - top), 0.0)
        iprob = expo / jnp.sum(expo, axis=1, keepdims=True)
        gradient = iprob - target
        dz_val = jnp.where(z_val > 0, gradient[:, None, :] * weight[:, :, None], 0.0).astype(jnp.bfloat16)
        dz_f = dz_val.astype(jnp.float32)
        dquery = (jnp.einsum('tjs,sd->tjd', dz_f, keys_f) * index_scale).astype(jnp.bfloat16)
        dkey = jnp.einsum('tjs,tjd->sd', dz_f, iquery.astype(jnp.float32)) * index_scale
        return carry + dkey, dquery

    start = jnp.zeros((KEYS, ID), jnp.float32)
    dkey, dquery = lax.scan(one_tile, start, (query_tiles, norm_tiles, iquery_tiles, weight_tiles, allow_cols))
    return dquery.reshape(QUERIES, IH, ID), dkey
```

```python
import functools

import jax
import jax.numpy as jnp
from jax import lax
from jax.experimental import pallas as pl
from jax.experimental.pallas import tpu as pltpu
from jax.sharding import PartitionSpec as P


attn_scale = 192.0 ** (-0.5)
LOG2E = 1.4426950408889634
STEPS = (1, 3, 2)
f32 = jnp.float32
bf16 = jnp.bfloat16
VM = pl.BlockSpec(memory_space=pltpu.VMEM)
SM = pl.BlockSpec(memory_space=pltpu.SMEM)


def along_y(value, d):
    return lax.ppermute(value, "seq", [(i, (i + 4 * d) % 16) for i in range(16)])


def along_z(value):
    return lax.ppermute(value, "seq", [(i, i ^ 2) for i in range(16)])


def other_core(value):
    return lax.ppermute(value, "seq", [(i, i ^ 1) for i in range(16)])


def along_x(value, d):
    return lax.ppermute(value, "head", [(i, i // 4 * 4 + (i + d) % 4) for i in range(16)])


def along_zh(value, d):
    return lax.ppermute(value, "head", [(i, (i + 4 * d) % 16) for i in range(16)])


def sds(shape, dtype):
    return jax.ShapeDtypeStruct(shape, dtype)


def call(body, outs, specs, **more):
    return pl.pallas_call(
        body,
        out_shape=outs,
        in_specs=specs,
        out_specs=jax.tree.map(lambda _: VM, outs),
        **more,
    )


def score_body(at_ref, q_ref, lse_ref, k0_ref, k1_ref, o0, o1, o2, o3, keys, acc):
    h = pl.program_id(0)
    rows = o0.shape[0]

    @pl.when(h == 0)
    def _():
        for v, ref in enumerate((k0_ref, k1_ref)):
            for u in range(2):
                keys[:, (2 * v + u) * 128 : (2 * v + u + 1) * 128] = ref[u, 128:, :]

    s = jnp.dot(q_ref[0], keys[...], preferred_element_type=f32)
    p = jnp.exp2(s * (attn_scale * LOG2E) - lse_ref[0] * LOG2E)

    @pl.when(h == 0)
    def _():
        acc[...] = p

    @pl.when(h > 0)
    def _():
        acc[...] += p

    @pl.when(h == pl.num_programs(0) - 1)
    def _():
        x = at_ref[1]
        for d, ref in zip((0,) + STEPS, (o0, o1, o2, o3)):
            at = pl.multiple_of(lax.rem(x + d, 4) * rows, rows)
            ref[...] = acc[pl.ds(at, rows), :].astype(ref.dtype)


def scores(at, query, lse, k0, k1):
    heads, rows, width = query.shape
    outs = (sds((rows // 4, 512), f32),) + (sds((rows // 4, 512), bf16),) * 3
    whole = lambda shape: pl.BlockSpec(shape, lambda h: (0,) * len(shape))
    return pl.pallas_call(
        score_body,
        grid=(heads,),
        out_shape=outs,
        in_specs=[
            SM,
            pl.BlockSpec((1, rows, width), lambda h: (h, 0, 0)),
            pl.BlockSpec((1, rows, 1), lambda h: (h, 0, 0)),
            whole(k0.shape),
            whole(k1.shape),
        ],
        out_specs=tuple(whole(o.shape) for o in outs),
        scratch_shapes=[pltpu.VMEM((width, 512), bf16), pltpu.VMEM((rows, 512), f32)],
        name="scores",
    )(at, query, lse, k0, k1)


def fold_body(at_ref, a0, a1, a2, a3, o0, o1, o2, o3, acc):
    acc[...] = a0[...] + a1[...].astype(f32) + a2[...].astype(f32) + a3[...].astype(f32)
    rows = o0.shape[0]
    for d, ref in zip((0,) + STEPS, (o0, o1, o2, o3)):
        at = pl.multiple_of(lax.rem(at_ref[0] + d, 4) * rows, rows)
        ref[...] = acc[pl.ds(at, rows), :].astype(ref.dtype)


def fold_over_x(at, parts):
    rows, cols = parts[0].shape
    outs = (sds((rows // 4, cols), f32),) + (sds((rows // 4, cols), bf16),) * 3
    return call(
        fold_body, outs, [SM] + [VM] * 4, scratch_shapes=[pltpu.VMEM((rows, cols), f32)], name="fold"
    )(at, *parts)


def pack_body(at_ref, q_ref, w_ref, o0, o1, o2, o3):
    for d, ref in zip((0,) + STEPS, (o0, o1, o2, o3)):
        x = lax.rem(at_ref[1] + d, 4)
        for b in range(4):
            ref[b, 0:64, :] = q_ref[x * 4 + b]
            ref[b, 64:80, :] = w_ref[x * 4 + b]


def spread_body(at_ref, a0, a1, a2, a3, o0, o1, o2, o3):
    for d, ref in zip((0,) + STEPS, (o0, o1, o2, o3)):
        zh = lax.rem(at_ref[0] + d, 4)
        for a, src in enumerate((a0, a1, a2, a3)):
            ref[a] = src[zh]


def turn_body(*refs):
    for e in range(4):
        for a in range(4):
            refs[4 + a][e] = refs[e][a]


def place_body(at_ref, a0, a1, a2, a3, out):
    for d, src in zip((0,) + STEPS, (a0, a1, a2, a3)):
        x = lax.rem(at_ref[1] + d, 4)
        for b, e in enumerate((0,) + STEPS):
            out[x * 4 + lax.rem(at_ref[0] + e, 4)] = src[b]


def weight_column(ref, a):
    row = jnp.sum(ref[a, 64:80, :].astype(f32), axis=0, keepdims=True)[:, 0:64]
    eye = lax.broadcasted_iota(jnp.int32, (64, 64), 0) == lax.broadcasted_iota(jnp.int32, (64, 64), 1)
    return jnp.sum(jnp.where(eye, row, 0.0), axis=1, keepdims=True)


def slot_tile(at_ref, slot):
    k, v, u = slot // 4, slot // 2 % 2, slot % 2
    y = lax.rem(at_ref[2] + ((0,) + STEPS)[k], 4)
    z = at_ref[3] if u == 0 else 1 - at_ref[3]
    c = at_ref[4] if v == 0 else 1 - at_ref[4]
    return y * 4 + z * 2 + c


def allowed(at_ref, kept_ref):
    half = jnp.where(at_ref[1] >= 2, 1, 0)
    flags = [
        jnp.full((16, 128), kept_ref[half, slot_tile(at_ref, slot)], jnp.int32) for slot in range(16)
    ]
    return jnp.concatenate(flags, axis=1) > 0


def gather_keys(k_refs, keys):
    for k in range(4):
        for v in range(2):
            for u in range(2):
                at = (k * 4 + v * 2 + u) * 128
                keys[at : at + 128, :] = k_refs[2 * k + v][u]


NT = (((1,), (1,)), ((), ()))
TN = (((0,), (0,)), ((), ()))


def index_body(scale, at_ref, kept_ref, *refs):
    q_refs, k_refs = refs[:4], refs[4:12]
    prob_ref, z_ref, keys, acc = refs[12:]
    gather_keys(k_refs, keys)
    for g, ref in enumerate(q_refs):
        rows = ref[:, 0:64, :].reshape(256, 128)
        z = lax.dot_general(rows, keys[...], NT, preferred_element_type=f32)
        z_ref[g] = z.astype(bf16)
        part = None
        for a in range(4):
            term = jnp.maximum(z[a * 64 : a * 64 + 64], 0.0) * (weight_column(ref, a) * scale)
            part = term if part is None else part + term
        if g == 0:
            acc[...] = part
        else:
            acc[...] += part
    pick = (
        lax.broadcasted_iota(jnp.int32, (16, 64), 1) // 4
        == lax.broadcasted_iota(jnp.int32, (16, 64), 0)
    ).astype(f32)
    logit = jnp.dot(pick, acc[...], precision=lax.Precision.HIGHEST, preferred_element_type=f32)
    keep = allowed(at_ref, kept_ref)
    top = jnp.max(jnp.where(keep, logit, -jnp.inf), axis=1, keepdims=True)
    expo = jnp.where(keep, jnp.exp(jnp.where(keep, logit, top) - top), 0.0)
    prob_ref[...] = expo / jnp.sum(expo, axis=1, keepdims=True)


def index_forward(at, kept, queries, keys, scale):
    outs = (sds((16, 2048), f32), sds((4, 256, 2048), bf16))
    key_spec = pl.BlockSpec((2, 128, 128), lambda i: (0, 0, 0))
    return call(
        functools.partial(index_body, scale),
        outs,
        [SM, SM] + [VM] * 4 + [key_spec] * 8,
        grid=(1,),
        scratch_shapes=[pltpu.VMEM((2048, 128), bf16), pltpu.VMEM((64, 2048), f32)],
        name="index_forward",
    )(at, kept, *queries, *keys)


def back_body(scale, at_ref, kept_ref, *refs):
    prob_ref, z_ref = refs[:2]
    q_refs, k_refs, s_refs = refs[2:6], refs[6:14], refs[14:30]
    own_ref, send_ref, dq_refs = refs[30], refs[31], refs[32:36]
    keys, grad, dz, dk = refs[36:]
    gather_keys(k_refs, keys)
    for k in range(4):
        a0, a1, a2, a3 = s_refs[4 * k : 4 * k + 4]
        grad[:, k * 512 : k * 512 + 512] = (
            a0[...] + a1[...].astype(f32) + a2[...].astype(f32) + a3[...].astype(f32)
        )
    head_sum = jnp.where(allowed(at_ref, kept_ref), grad[...], 0.0)
    grad[...] = prob_ref[...] - head_sum / jnp.sum(head_sum, axis=1, keepdims=True)
    pick = (
        lax.broadcasted_iota(jnp.int32, (64, 16), 0) // 4
        == lax.broadcasted_iota(jnp.int32, (64, 16), 1)
    ).astype(f32)
    wide = jnp.dot(pick, grad[...], precision=lax.Precision.HIGHEST, preferred_element_type=f32)
    for g, ref in enumerate(q_refs):
        for a in range(4):
            at = a * 64
            dz[at : at + 64, :] = jnp.where(
                z_ref[g, at : at + 64, :].astype(f32) > 0.0, wide * weight_column(ref, a), 0.0
            ).astype(bf16)
        rows = ref[:, 0:64, :].reshape(256, 128)
        part = lax.dot_general(rows, dz[...], TN, preferred_element_type=f32)
        if g == 0:
            dk[...] = part
        else:
            dk[...] += part
        dq = jnp.dot(dz[...], keys[...], preferred_element_type=f32) * scale
        dq_refs[g][...] = dq.astype(bf16).reshape(4, 64, 128)
    for k in range(4):
        for u in range(2):
            at = (k * 4 + u) * 128
            own_ref[k, u] = dk[:, at : at + 128] * scale
            at = (k * 4 + 2 + u) * 128
            send_ref[k, u] = (dk[:, at : at + 128] * scale).astype(bf16)


def index_backward(at, kept, prob, z, queries, keys, sums, scale):
    outs = (sds((4, 2, 128, 128), f32), sds((4, 2, 128, 128), bf16)) + (sds((4, 64, 128), bf16),) * 4
    key_spec = pl.BlockSpec((2, 128, 128), lambda i: (0, 0, 0))
    return call(
        functools.partial(back_body, scale),
        outs,
        [SM, SM, VM, VM] + [VM] * 4 + [key_spec] * 8 + [VM] * 16,
        grid=(1,),
        scratch_shapes=[
            pltpu.VMEM((2048, 128), bf16),
            pltpu.VMEM((16, 2048), f32),
            pltpu.VMEM((256, 2048), bf16),
            pltpu.VMEM((128, 2048), f32),
        ],
        name="index_backward",
    )(at, kept, prob, z, *queries, *keys, *sums)


def core_sum_body(own, got, o0, o1, o2, o3):
    for k, ref in enumerate((o0, o1, o2, o3)):
        ref[...] = (own[k] + got[k].astype(f32)).astype(ref.dtype)


def y_sum_body(a0, a1, a2, a3, keep, send):
    for u, ref in enumerate((keep, send)):
        total = a0[u] + a1[u].astype(f32) + a2[u].astype(f32) + a3[u].astype(f32)
        ref[...] = total.astype(ref.dtype)


def z_sum_body(a0, a1, send):
    send[...] = (a0[...] + a1[...].astype(f32)).astype(bf16)


def ring_sum(a0, a1, a2, a3):
    return (a0[...].astype(f32) + a3[...].astype(f32)) + (a1[...].astype(f32) + a2[...].astype(f32))


def x_sum_body(a0, a1, a2, a3, send):
    send[...] = ring_sum(a0, a1, a2, a3).astype(bf16)


def last_sum_body(a0, a1, a2, a3, out):
    out[...] = ring_sum(a0, a1, a2, a3).T


def key_gradient(own, send):
    got = other_core(send)
    pair = (2, 128, 128)
    tile = (128, 128)
    parts = call(
        core_sum_body, (sds(pair, f32),) + (sds(pair, bf16),) * 3, [VM] * 2, name="core_sum"
    )(own, got)
    parts = [parts[0]] + [along_y(p, d) for p, d in zip(parts[1:], STEPS)]
    keep, send = call(y_sum_body, (sds(tile, f32), sds(tile, bf16)), [VM] * 4, name="y_sum")(*parts)
    send = call(z_sum_body, sds(tile, bf16), [VM] * 2, name="z_sum")(keep, along_z(send))
    send = call(x_sum_body, sds(tile, bf16), [VM] * 4, name="x_sum")(
        send, *[along_x(send, d) for d in STEPS]
    )
    return call(last_sum_body, sds(tile, f32), [VM] * 4, name="last_sum")(
        send, *[along_zh(send, d) for d in STEPS]
    )


def local(query_latent, key_latent, normalizer, index_query, index_key, index_weight, kept):
    query_rows, head_count, width = query_latent.shape
    index_scale = index_query.shape[2] ** (-0.5)
    head = lax.axis_index("head")
    seq = lax.axis_index("seq")
    at = jnp.stack([head // 4, head % 4, seq // 4, seq // 2 % 2, seq % 2]).astype(jnp.int32)

    tile = jnp.concatenate([index_key, key_latent.T], axis=0)
    pairs = [jnp.stack([tile, along_z(tile)])]
    pairs += [along_y(pairs[0], -d) for d in STEPS]
    keys = []
    for pair in pairs:
        keys += [pair, other_core(pair)]

    w0 = lax.reduce_precision(index_weight, 8, 7)
    w1 = lax.reduce_precision(index_weight - w0, 8, 7)
    w2 = index_weight - w0 - w1
    weight = jnp.stack([w.reshape(16, 64) for w in (w0, w1, w2)], axis=1).astype(bf16)
    weight = jnp.pad(weight, ((0, 0), (0, 13), (0, 64)))
    four = (sds((4, 80, 128), bf16),) * 4
    parts = call(pack_body, four, [SM, VM, VM], name="pack")(
        at, index_query.reshape(16, 64, 128), weight
    )
    parts = [parts[0]] + [along_x(p, d) for p, d in zip(parts[1:], STEPS)]
    parts = call(spread_body, four, [SM] + [VM] * 4, name="spread")(at, *parts)
    queries = [parts[0]] + [along_zh(p, d) for p, d in zip(parts[1:], STEPS)]

    query = jnp.transpose(query_latent, (1, 0, 2))
    lse = normalizer.T[:, :, None]
    sums = []
    for k in range(4):
        parts = scores(at, query, lse, keys[2 * k], keys[2 * k + 1])
        parts = [parts[0]] + [along_x(p, d) for p, d in zip(parts[1:], STEPS)]
        parts = fold_over_x(at, parts)
        sums += [parts[0]] + [along_zh(p, d) for p, d in zip(parts[1:], STEPS)]

    prob, z = index_forward(at, kept, queries, keys, index_scale)
    own, send, *dq = index_backward(at, kept, prob, z, queries, keys, sums, index_scale)
    dkey = key_gradient(own, send)

    block = (sds((4, 64, 128), bf16),) * 4
    dq = [dq[0]] + [along_zh(p, -d) for p, d in zip(dq[1:], STEPS)]
    dq = call(turn_body, block, [VM] * 4, name="turn")(*dq)
    dq = [dq[0]] + [along_x(p, -d) for p, d in zip(dq[1:], STEPS)]
    dquery = call(place_body, sds((16, 64, 128), bf16), [SM] + [VM] * 4, name="place")(at, *dq)
    return dquery.reshape(index_query.shape), dkey


def solution(mesh):
    return jax.shard_map(
        local,
        mesh=mesh,
        in_specs=(
            P("seq", "head", None),
            P("seq", None),
            P("seq", "head"),
            P("seq", "head", None),
            P("seq", None),
            P("seq", "head"),
            P("seq", None),
        ),
        out_specs=(P("seq", "head", None), P("seq", None)),
        check_vma=False,
    )
```

```python
import functools

import jax
import jax.numpy as jnp
from jax import lax
from jax.experimental import pallas as pl
from jax.experimental.pallas import tpu as pltpu
from jax.sharding import PartitionSpec as P


attn_scale = 192.0 ** (-0.5)
LOG2E = 1.4426950408889634
STEPS = (1, 3, 2)
GROUPS = ((0, 1), (2, 3))
f32 = jnp.float32
bf16 = jnp.bfloat16
VM = pl.BlockSpec(memory_space=pltpu.VMEM)
SM = pl.BlockSpec(memory_space=pltpu.SMEM)

ROW_X = [[zh * 4 + x for x in range(4)] for zh in range(4)]
ROW_ZH = [[zh * 4 + x for zh in range(4)] for x in range(4)]
SAME_CORE = [[i * 2 + c for i in range(8)] for c in range(2)]


def along_y(value, d):
    return lax.ppermute(value, "seq", [(i, (i + 4 * d) % 16) for i in range(16)])


def along_z(value):
    return lax.ppermute(value, "seq", [(i, i ^ 2) for i in range(16)])


def other_core(value):
    return lax.ppermute(value, "seq", [(i, i ^ 1) for i in range(16)])


def exchanged(value, axis, groups=None):
    return lax.all_to_all(value, axis, 0, 0, tiled=True, axis_index_groups=groups)


def summed_copies(value, axis, groups):
    count = len(groups[0])
    copies = jnp.broadcast_to(value, (count, *value.shape))
    return jnp.sum(exchanged(copies, axis, groups).astype(f32), axis=0)


def sds(shape, dtype):
    return jax.ShapeDtypeStruct(shape, dtype)


def call(body, outs, specs, **more):
    return pl.pallas_call(
        body,
        out_shape=outs,
        in_specs=specs,
        out_specs=jax.tree.map(lambda _: VM, outs),
        **more,
    )


def query_body(q_ref, lse_ref, out_ref, wide):
    h = pl.program_id(0)
    width = q_ref.shape[1]
    value = lse_ref[pl.ds(h, 1), :] * (-1.0 / attn_scale)
    p0 = value.astype(bf16).astype(f32)
    p1 = (value - p0).astype(bf16).astype(f32)
    p2 = value - p0 - p1
    row = lax.broadcasted_iota(jnp.int32, (wide.shape[0] - width, wide.shape[1]), 0)
    more = jnp.where(row == 0, p0, jnp.where(row == 1, p1, jnp.where(row == 2, p2, 0.0)))
    wide[0:width, :] = q_ref[0]
    wide[width:, :] = more.astype(bf16)
    out_ref[0] = wide[...].T


def wide_queries(query, normalizer):
    heads, width, rows = query.shape
    return pl.pallas_call(
        query_body,
        grid=(heads,),
        out_shape=sds((heads, rows, 640), bf16),
        in_specs=[
            pl.BlockSpec((1, width, rows), lambda h: (h, 0, 0)),
            pl.BlockSpec((heads, rows), lambda h: (0, 0)),
        ],
        out_specs=pl.BlockSpec((1, rows, 640), lambda h: (h, 0, 0)),
        scratch_shapes=[pltpu.VMEM((640, rows), bf16)],
        name="wide_queries",
    )(query, normalizer)


def score_body(q_ref, *refs):
    k_refs, out_ref, keys = refs[:-2], refs[-2], refs[-1]
    n = pl.program_id(0)
    heads, rows, _ = q_ref.shape
    width = k_refs[0].shape[1]

    @pl.when(n == 0)
    def _():
        row = lax.broadcasted_iota(jnp.int32, (keys.shape[0] - width, 256), 0)
        keys[width:, :] = jnp.where(row < 3, 1.0, 0.0).astype(bf16)

    for i, ref in enumerate(k_refs):

        @pl.when(n == i)
        def _():
            for u in range(2):
                keys[0:width, u * 128 : u * 128 + 128] = ref[u]

    total = None
    for h in range(0, heads, 2):
        both = q_ref[h : h + 2].reshape(2 * rows, q_ref.shape[2])
        s = jnp.dot(both, keys[...], preferred_element_type=f32)
        p = jnp.exp2(s * (attn_scale * LOG2E))
        p = p[:rows] + p[rows:]
        total = p if total is None else total + p
    out_ref[...] = total.astype(bf16)


def scores(query, pairs):
    heads, rows, wide = query.shape
    whole = lambda shape: pl.BlockSpec(shape, lambda n: (0,) * len(shape))
    return pl.pallas_call(
        score_body,
        grid=(len(pairs),),
        out_shape=sds((rows, 256 * len(pairs)), bf16),
        in_specs=[whole(query.shape)] + [whole(p.shape) for p in pairs],
        out_specs=pl.BlockSpec((rows, 256), lambda n: (0, n)),
        scratch_shapes=[pltpu.VMEM((wide, 256), bf16)],
        name="scores",
    )(query, *pairs)


def weight_column(q_ref, j):
    row = jnp.sum(q_ref[j, 64:80, :].astype(f32), axis=0, keepdims=True)[:, 0:64]
    eye = lax.broadcasted_iota(jnp.int32, (64, 64), 0) == lax.broadcasted_iota(jnp.int32, (64, 64), 1)
    return jnp.sum(jnp.where(eye, row, 0.0), axis=1, keepdims=True)


def slot_tile(at_ref, slot):
    k, v, u = slot // 4, slot // 2 % 2, slot % 2
    y = lax.rem(at_ref[1] + ((0,) + STEPS)[k], 4)
    z = at_ref[2] if u == 0 else 1 - at_ref[2]
    c = at_ref[3] if v == 0 else 1 - at_ref[3]
    return y * 4 + z * 2 + c


def allowed(at_ref, kept_ref):
    half = jnp.where(at_ref[0] >= 8, 1, 0)
    flags = [
        jnp.full((16, 128), kept_ref[half, slot_tile(at_ref, slot)], jnp.int32) for slot in range(16)
    ]
    return jnp.concatenate(flags, axis=1) > 0


def gather_keys(at_ref, k_ref, keys):
    for slot in range(16):
        keys[slot * 128 : slot * 128 + 128, :] = k_ref[slot_tile(at_ref, slot)]


NT = (((1,), (1,)), ((), ()))
TN = (((0,), (0,)), ((), ()))


def index_body(scale, at_ref, kept_ref, q_ref, k_ref, prob_ref, z_ref, keys, acc):
    gather_keys(at_ref, k_ref, keys)
    acc[...] = jnp.zeros_like(acc)

    @pl.loop(0, 4)
    def _(g):
        rows = q_ref[pl.ds(4 * g, 4), 0:64, :].reshape(256, 128)
        z = lax.dot_general(rows, keys[...], NT, preferred_element_type=f32)
        z_ref[g] = z.astype(bf16)
        part = None
        for a in range(4):
            weight = weight_column(q_ref, 4 * g + a) * scale
            term = jnp.maximum(z[a * 64 : a * 64 + 64], 0.0) * weight
            part = term if part is None else part + term
        acc[...] += part

    pick = (
        lax.broadcasted_iota(jnp.int32, (16, 64), 1) // 4
        == lax.broadcasted_iota(jnp.int32, (16, 64), 0)
    ).astype(f32)
    logit = jnp.dot(pick, acc[...], precision=lax.Precision.HIGHEST, preferred_element_type=f32)
    keep = allowed(at_ref, kept_ref)
    top = jnp.max(jnp.where(keep, logit, -jnp.inf), axis=1, keepdims=True)
    expo = jnp.where(keep, jnp.exp(jnp.where(keep, logit, top) - top), 0.0)
    prob_ref[...] = expo / jnp.sum(expo, axis=1, keepdims=True)


def index_forward(at, kept, queries, keys, scale):
    return call(
        functools.partial(index_body, scale),
        (sds((16, 2048), f32), sds((4, 256, 2048), bf16)),
        [SM, SM, VM, VM],
        scratch_shapes=[pltpu.VMEM((2048, 128), bf16), pltpu.VMEM((64, 2048), f32)],
        name="index_forward",
    )(at, kept, queries, keys)


def fill_dz(g, wide, z_ref, q_ref, dz):
    for a in range(4):
        at = a * 64
        dz[at : at + 64, :] = jnp.where(
            z_ref[g, at : at + 64, :].astype(f32) > 0.0, wide * weight_column(q_ref, 4 * g + a), 0.0
        ).astype(bf16)


def repeated(grad):
    pick = (
        lax.broadcasted_iota(jnp.int32, (64, 16), 0) // 4
        == lax.broadcasted_iota(jnp.int32, (64, 16), 1)
    ).astype(f32)
    return jnp.dot(pick, grad, precision=lax.Precision.HIGHEST, preferred_element_type=f32)


def key_grad_body(scale, at_ref, kept_ref, prob_ref, z_ref, q_ref, *refs):
    sums, (own_ref, send_ref, grad_ref, dz, dk, wide) = refs[:-6], refs[-6:]
    begin = 0
    for ref in sums:
        total = ref[0].astype(f32)
        for j in range(1, 16):
            total += ref[j].astype(f32)
        grad_ref[:, begin : begin + ref.shape[2]] = total
        begin += ref.shape[2]
    head_sum = jnp.where(allowed(at_ref, kept_ref), grad_ref[...], 0.0)
    grad_ref[...] = prob_ref[...] - head_sum / jnp.sum(head_sum, axis=1, keepdims=True)
    wide[...] = repeated(grad_ref[...])
    dk[...] = jnp.zeros_like(dk)

    @pl.loop(0, 4)
    def _(g):
        fill_dz(g, wide[...], z_ref, q_ref, dz)
        rows = q_ref[pl.ds(4 * g, 4), 0:64, :].reshape(256, 128)
        dk[...] += lax.dot_general(rows, dz[...], TN, preferred_element_type=f32)

    for slot in range(16):
        tile = dk[:, slot * 128 : slot * 128 + 128] * scale
        place = lax.div(slot_tile(at_ref, slot), 2)
        if slot // 2 % 2 == 0:
            own_ref[place] = tile
        else:
            send_ref[place] = tile.astype(bf16)


def key_grad(at, kept, prob, z, queries, sums, scale):
    return call(
        functools.partial(key_grad_body, scale),
        (sds((8, 128, 128), f32), sds((8, 128, 128), bf16), sds((16, 2048), f32)),
        [SM, SM] + [VM] * (3 + len(sums)),
        scratch_shapes=[
            pltpu.VMEM((256, 2048), bf16),
            pltpu.VMEM((128, 2048), f32),
            pltpu.VMEM((64, 2048), f32),
        ],
        name="key_grad",
    )(at, kept, prob, z, queries, *sums)


def query_grad_body(scale, at_ref, grad_ref, z_ref, q_ref, k_ref, out_ref, keys, dz, wide):
    gather_keys(at_ref, k_ref, keys)
    wide[...] = repeated(grad_ref[...])

    @pl.loop(0, 4)
    def _(g):
        fill_dz(g, wide[...], z_ref, q_ref, dz)
        dq = jnp.dot(dz[...], keys[...], preferred_element_type=f32) * scale
        out_ref[pl.ds(4 * g, 4)] = dq.astype(bf16).reshape(4, 64, 128)


def query_grad(at, grad, z, queries, keys, scale):
    return call(
        functools.partial(query_grad_body, scale),
        sds((16, 64, 128), bf16),
        [SM] + [VM] * 4,
        scratch_shapes=[
            pltpu.VMEM((2048, 128), bf16),
            pltpu.VMEM((256, 2048), bf16),
            pltpu.VMEM((64, 2048), f32),
        ],
        name="query_grad",
    )(at, grad, z, queries, keys)


def local(query_latent, key_latent, normalizer, index_query, index_key, index_weight, kept):
    index_scale = index_query.shape[2] ** (-0.5)
    head = lax.axis_index("head")
    seq = lax.axis_index("seq")
    at = jnp.stack([head, seq // 4, seq // 2 % 2, seq % 2]).astype(jnp.int32)

    tile = key_latent.T
    pairs = [jnp.stack([tile, along_z(tile)])]
    pairs += [along_y(pairs[0], -d) for d in STEPS]
    index_keys = exchanged(jnp.broadcast_to(index_key, (16, *index_key.shape)), "seq")

    w0 = lax.reduce_precision(index_weight, 8, 7)
    w1 = lax.reduce_precision(index_weight - w0, 8, 7)
    w2 = index_weight - w0 - w1
    weight = jnp.stack([w.reshape(16, 64) for w in (w0, w1, w2)], axis=1).astype(bf16)
    weight = jnp.pad(weight, ((0, 0), (0, 13), (0, 64)))
    queries = exchanged(jnp.concatenate([index_query.reshape(16, 64, 128), weight], axis=1), "head")

    query = wide_queries(jnp.transpose(query_latent, (1, 2, 0)), normalizer.T)
    sums = []
    for group in GROUPS:
        part = scores(query, [p for k in group for p in (pairs[k], other_core(pairs[k]))])
        sums.append(exchanged(part.reshape(16, 16, part.shape[1]), "head"))

    prob, z = index_forward(at, kept, queries, index_keys, index_scale)
    own, send, grad = key_grad(at, kept, prob, z, queries, sums, index_scale)

    dkey = (own + other_core(send).astype(f32)).astype(bf16)
    dkey = jnp.sum(exchanged(dkey, "seq", SAME_CORE).astype(f32), axis=0).astype(bf16)
    dkey = summed_copies(dkey, "head", ROW_X).astype(bf16)
    dkey = summed_copies(dkey, "head", ROW_ZH).T

    dquery = exchanged(query_grad(at, grad, z, queries, index_keys, index_scale), "head")
    return dquery.reshape(index_query.shape), dkey


def solution(mesh):
    return jax.shard_map(
        local,
        mesh=mesh,
        in_specs=(
            P("seq", "head", None),
            P("seq", None),
            P("seq", "head"),
            P("seq", "head", None),
            P("seq", None),
            P("seq", "head"),
            P("seq", None),
        ),
        out_specs=(P("seq", "head", None), P("seq", None)),
        check_vma=False,
    )
```

```python
import functools

import jax
import jax.numpy as jnp
from jax import lax
from jax.experimental import pallas as pl
from jax.experimental.pallas import tpu as pltpu
from jax.sharding import PartitionSpec as P


attn_scale = 192.0 ** (-0.5)
LOG2E = 1.4426950408889634
STEPS = (1, 3, 2)
GROUPS = ((0, 1), (2, 3))
f32 = jnp.float32
bf16 = jnp.bfloat16
VM = pl.BlockSpec(memory_space=pltpu.VMEM)
SM = pl.BlockSpec(memory_space=pltpu.SMEM)

ROW_X = [[zh * 4 + x for x in range(4)] for zh in range(4)]
ROW_ZH = [[zh * 4 + x for zh in range(4)] for x in range(4)]
YZX = [
    [(y * 4 + z * 2 + c) * 16 + zh * 4 + x for y in range(4) for z in range(2) for x in range(4)]
    for zh in range(4)
    for c in range(2)
]


def along_y(value, d):
    return lax.ppermute(value, "seq", [(i, (i + 4 * d) % 16) for i in range(16)])


def along_z(value):
    return lax.ppermute(value, "seq", [(i, i ^ 2) for i in range(16)])


def other_core(value):
    return lax.ppermute(value, "seq", [(i, i ^ 1) for i in range(16)])


def exchanged(value, axis, groups=None):
    return lax.all_to_all(value, axis, 0, 0, tiled=True, axis_index_groups=groups)


def sds(shape, dtype):
    return jax.ShapeDtypeStruct(shape, dtype)


def call(body, outs, specs, **more):
    return pl.pallas_call(
        body,
        out_shape=outs,
        in_specs=specs,
        out_specs=jax.tree.map(lambda _: VM, outs),
        **more,
    )


def query_body(q_ref, lse_ref, out_ref, wide):
    h = pl.program_id(0)
    width = q_ref.shape[1]
    value = lse_ref[pl.ds(h, 1), :] * (-1.0 / attn_scale)
    p0 = value.astype(bf16).astype(f32)
    p1 = (value - p0).astype(bf16).astype(f32)
    p2 = value - p0 - p1
    row = lax.broadcasted_iota(jnp.int32, (wide.shape[0] - width, wide.shape[1]), 0)
    more = jnp.where(row == 0, p0, jnp.where(row == 1, p1, jnp.where(row == 2, p2, 0.0)))
    wide[0:width, :] = q_ref[0]
    wide[width:, :] = more.astype(bf16)
    out_ref[0] = wide[...].T


def wide_queries(query, normalizer):
    heads, width, rows = query.shape
    return pl.pallas_call(
        query_body,
        grid=(heads,),
        out_shape=sds((heads, rows, 640), bf16),
        in_specs=[
            pl.BlockSpec((1, width, rows), lambda h: (h, 0, 0)),
            pl.BlockSpec((heads, rows), lambda h: (0, 0)),
        ],
        out_specs=pl.BlockSpec((1, rows, 640), lambda h: (h, 0, 0)),
        scratch_shapes=[pltpu.VMEM((640, rows), bf16)],
        name="wide_queries",
    )(query, normalizer)


def score_body(q_ref, *refs):
    k_refs, out_ref, keys = refs[:-2], refs[-2], refs[-1]
    k_refs = [ref for ref in k_refs if len(ref.shape) == 3]
    n = pl.program_id(0)
    heads, rows, _ = q_ref.shape
    width = k_refs[0].shape[1] - 128

    @pl.when(n == 0)
    def _():
        row = lax.broadcasted_iota(jnp.int32, (keys.shape[0] - width, 256), 0)
        keys[width:, :] = jnp.where(row < 3, 1.0, 0.0).astype(bf16)

    for i, ref in enumerate(k_refs):

        @pl.when(n == i)
        def _():
            for u in range(2):
                keys[0:width, u * 128 : u * 128 + 128] = ref[u, 128:, :]

    total = None
    for h in range(0, heads, 2):
        both = q_ref[h : h + 2].reshape(2 * rows, q_ref.shape[2])
        s = jnp.dot(both, keys[...], preferred_element_type=f32)
        p = jnp.exp2(s * (attn_scale * LOG2E))
        p = p[:rows] + p[rows:]
        total = p if total is None else total + p
    for x in range(4):
        for zh in range(4):
            at, begin = (x * 4 + zh) * 16, (zh * 4 + x) * 16
            out_ref[at : at + 16, :] = total[begin : begin + 16].astype(bf16)


def scores(query, pairs, into, begin):
    _, rows, wide = query.shape
    whole = lambda shape: pl.BlockSpec(shape, lambda n: (0,) * len(shape))
    more = () if into is None else (into,)
    return pl.pallas_call(
        score_body,
        grid=(len(pairs),),
        out_shape=sds((rows, 2048), bf16),
        in_specs=[whole(query.shape)]
        + [whole(p.shape) for p in pairs]
        + [pl.BlockSpec(memory_space=pl.ANY) for _ in more],
        out_specs=pl.BlockSpec((rows, 256), lambda n: (0, n + begin)),
        scratch_shapes=[pltpu.VMEM((wide, 256), bf16)],
        input_output_aliases={1 + len(pairs): 0} if more else {},
        name="scores",
    )(query, *pairs, *more)


def weight_column(q_ref, j):
    row = jnp.sum(q_ref[j, 64:80, :].astype(f32), axis=0, keepdims=True)[:, 0:64]
    eye = lax.broadcasted_iota(jnp.int32, (64, 64), 0) == lax.broadcasted_iota(jnp.int32, (64, 64), 1)
    return jnp.sum(jnp.where(eye, row, 0.0), axis=1, keepdims=True)


def slot_tile(at_ref, slot):
    k, v, u = slot // 4, slot // 2 % 2, slot % 2
    y = lax.rem(at_ref[1] + ((0,) + STEPS)[k], 4)
    z = at_ref[2] if u == 0 else 1 - at_ref[2]
    c = at_ref[3] if v == 0 else 1 - at_ref[3]
    return y * 4 + z * 2 + c


def allowed(at_ref, kept_ref):
    half = jnp.where(at_ref[0] >= 8, 1, 0)
    flags = [
        jnp.full((16, 128), kept_ref[half, slot_tile(at_ref, slot)], jnp.int32) for slot in range(16)
    ]
    return jnp.concatenate(flags, axis=1) > 0


KEY_SPEC = pl.BlockSpec((2, 128, 128), lambda i: (0, 0, 0))


def gather_keys(k_refs, keys):
    for slot in range(16):
        keys[slot * 128 : slot * 128 + 128, :] = k_refs[slot // 2][slot % 2]


NT = (((1,), (1,)), ((), ()))
TN = (((0,), (0,)), ((), ()))


def index_body(scale, at_ref, kept_ref, q_ref, *refs):
    k_refs, (prob_ref, z_ref, keys, acc) = refs[:8], refs[8:]
    gather_keys(k_refs, keys)
    acc[...] = jnp.zeros_like(acc)

    @pl.loop(0, 4)
    def _(g):
        rows = q_ref[pl.ds(4 * g, 4), 0:64, :].reshape(256, 128)
        z = lax.dot_general(rows, keys[...], NT, preferred_element_type=f32)
        z_ref[g] = z.astype(bf16)
        part = None
        for a in range(4):
            weight = weight_column(q_ref, 4 * g + a) * scale
            term = jnp.maximum(z[a * 64 : a * 64 + 64], 0.0) * weight
            part = term if part is None else part + term
        acc[...] += part

    pick = (
        lax.broadcasted_iota(jnp.int32, (16, 64), 1) // 4
        == lax.broadcasted_iota(jnp.int32, (16, 64), 0)
    ).astype(f32)
    logit = jnp.dot(pick, acc[...], precision=lax.Precision.HIGHEST, preferred_element_type=f32)
    keep = allowed(at_ref, kept_ref)
    top = jnp.max(jnp.where(keep, logit, -jnp.inf), axis=1, keepdims=True)
    expo = jnp.where(keep, jnp.exp(jnp.where(keep, logit, top) - top), 0.0)
    prob_ref[...] = expo / jnp.sum(expo, axis=1, keepdims=True)


def index_forward(at, kept, queries, keys, scale):
    return call(
        functools.partial(index_body, scale),
        (sds((16, 2048), f32), sds((4, 256, 2048), bf16)),
        [SM, SM, VM] + [KEY_SPEC] * 8,
        grid=(1,),
        scratch_shapes=[pltpu.VMEM((2048, 128), bf16), pltpu.VMEM((64, 2048), f32)],
        name="index_forward",
    )(at, kept, queries, *keys)


def fill_dz(g, wide, z_ref, q_ref, dz):
    for a in range(4):
        at = a * 64
        dz[at : at + 64, :] = jnp.where(
            z_ref[g, at : at + 64, :].astype(f32) > 0.0, wide * weight_column(q_ref, 4 * g + a), 0.0
        ).astype(bf16)


def repeated(grad):
    pick = (
        lax.broadcasted_iota(jnp.int32, (64, 16), 0) // 4
        == lax.broadcasted_iota(jnp.int32, (64, 16), 1)
    ).astype(f32)
    return jnp.dot(pick, grad, precision=lax.Precision.HIGHEST, preferred_element_type=f32)


def back_body(scale, at_ref, kept_ref, prob_ref, z_ref, q_ref, *refs):
    k_refs, refs = refs[:8], refs[8:]
    sums, (own_ref, send_ref, dq_ref, keys, grad, dz, dk, wide) = refs[:-8], refs[-8:]
    gather_keys(k_refs, keys)
    begin = 0
    for ref in sums:
        total = ref[0].astype(f32)
        for j in range(1, ref.shape[0]):
            total += ref[j].astype(f32)
        grad[:, begin : begin + ref.shape[2]] = total
        begin += ref.shape[2]
    head_sum = jnp.where(allowed(at_ref, kept_ref), grad[...], 0.0)
    wide[...] = repeated(prob_ref[...] - head_sum / jnp.sum(head_sum, axis=1, keepdims=True))
    dk[...] = jnp.zeros_like(dk)

    @pl.loop(0, 4)
    def _(g):
        fill_dz(g, wide[...], z_ref, q_ref, dz)
        rows = q_ref[pl.ds(4 * g, 4), 0:64, :].reshape(256, 128)
        dk[...] += lax.dot_general(rows, dz[...], TN, preferred_element_type=f32)
        dq = jnp.dot(dz[...], keys[...], preferred_element_type=f32) * scale
        dq_ref[pl.ds(4 * g, 4)] = dq.astype(bf16).reshape(4, 64, 128)

    for slot in range(16):
        tile = dk[:, slot * 128 : slot * 128 + 128] * scale
        place = lax.div(slot_tile(at_ref, slot), 2)
        if slot // 2 % 2 == 0:
            own_ref[place] = tile
        else:
            send_ref[place] = tile.astype(bf16)


def index_backward(at, kept, prob, z, queries, keys, sums, scale):
    return call(
        functools.partial(back_body, scale),
        (sds((8, 128, 128), f32), sds((8, 128, 128), bf16), sds((16, 64, 128), bf16)),
        [SM, SM] + [VM] * 3 + [KEY_SPEC] * 8 + [VM] * len(sums),
        grid=(1,),
        scratch_shapes=[
            pltpu.VMEM((2048, 128), bf16),
            pltpu.VMEM((16, 2048), f32),
            pltpu.VMEM((256, 2048), bf16),
            pltpu.VMEM((128, 2048), f32),
            pltpu.VMEM((64, 2048), f32),
        ],
        name="index_backward",
    )(at, kept, prob, z, queries, *keys, *sums)


def local(query_latent, key_latent, normalizer, index_query, index_key, index_weight, kept):
    index_scale = index_query.shape[2] ** (-0.5)
    head = lax.axis_index("head")
    seq = lax.axis_index("seq")
    at = jnp.stack([head, seq // 4, seq // 2 % 2, seq % 2]).astype(jnp.int32)

    tile = jnp.concatenate([index_key, key_latent.T], axis=0)
    other = along_z(tile)
    pairs = [jnp.stack([tile, other])]
    for d in STEPS:
        pairs.append(along_y(pairs[0], -d))
    keys = []
    for pair in pairs:
        keys += [pair, other_core(pair)]

    w0 = lax.reduce_precision(index_weight, 8, 7)
    w1 = lax.reduce_precision(index_weight - w0, 8, 7)
    w2 = index_weight - w0 - w1
    weight = jnp.stack([w.reshape(16, 64) for w in (w0, w1, w2)], axis=1).astype(bf16)
    weight = jnp.pad(weight, ((0, 0), (0, 13), (0, 64)))
    queries = jnp.concatenate([index_query.reshape(16, 64, 128), weight], axis=1)
    queries = exchanged(queries, "head")

    query = wide_queries(jnp.transpose(query_latent, (1, 2, 0)), normalizer.T)
    part, begin = None, 0
    for group in GROUPS:
        pieces = [p for k in group for p in keys[2 * k : 2 * k + 2]]
        part = scores(query, pieces, part, begin)
        begin += len(pieces)
    part = exchanged(part.reshape(4, 64, 2048), "head", ROW_X)
    part = jnp.sum(part.astype(f32), axis=0).astype(bf16)
    sums = exchanged(part.reshape(4, 16, 2048), "head", ROW_ZH)

    prob, z = index_forward(at, kept, queries, keys, index_scale)
    own, send, dq = index_backward(at, kept, prob, z, queries, keys, [sums], index_scale)

    got = other_core(send)
    dkey = (own + got.astype(f32)).astype(bf16)
    dkey = exchanged(dkey.reshape(32, 32, 128), ("seq", "head"), YZX)
    dkey = jnp.sum(dkey.astype(f32), axis=0).astype(bf16)
    dkey = jnp.broadcast_to(dkey, (16, 32, 128))
    both = exchanged(jnp.concatenate([dq, dkey], axis=1), "head")
    dkey = both[:, 64:].astype(f32).reshape(4, 4, 32, 128).sum(axis=0).reshape(128, 128).T
    return both[:, :64].reshape(index_query.shape), dkey


def solution(mesh):
    return jax.shard_map(
        local,
        mesh=mesh,
        in_specs=(
            P("seq", "head", None),
            P("seq", None),
            P("seq", "head"),
            P("seq", "head", None),
            P("seq", None),
            P("seq", "head"),
            P("seq", None),
        ),
        out_specs=(P("seq", "head", None), P("seq", None)),
        check_vma=False,
    )
```

```python
import functools

import jax
import jax.numpy as jnp
from jax import lax
from jax.experimental import pallas as pl
from jax.experimental.pallas import tpu as pltpu
from jax.sharding import PartitionSpec as P


attn_scale = 192.0 ** (-0.5)
LOG2E = 1.4426950408889634
STEPS = (1, 3, 2)
f32 = jnp.float32
bf16 = jnp.bfloat16
VM = pl.BlockSpec(memory_space=pltpu.VMEM)
SM = pl.BlockSpec(memory_space=pltpu.SMEM)

ROW_X = [[zh * 4 + x for x in range(4)] for zh in range(4)]
ROW_ZH = [[zh * 4 + x for zh in range(4)] for x in range(4)]
YZX = [
    [(y * 4 + z * 2 + c) * 16 + zh * 4 + x for y in range(4) for z in range(2) for x in range(4)]
    for zh in range(4)
    for c in range(2)
]


def along_y(value, d):
    return lax.ppermute(value, "seq", [(i, (i + 4 * d) % 16) for i in range(16)])


def along_z(value):
    return lax.ppermute(value, "seq", [(i, i ^ 2) for i in range(16)])


def other_core(value):
    return lax.ppermute(value, "seq", [(i, i ^ 1) for i in range(16)])


def exchanged(value, axis, groups=None):
    return lax.all_to_all(value, axis, 0, 0, tiled=True, axis_index_groups=groups)


def sds(shape, dtype):
    return jax.ShapeDtypeStruct(shape, dtype)


def call(body, outs, specs, mib, **more):
    return pl.pallas_call(
        body,
        out_shape=outs,
        in_specs=specs,
        out_specs=jax.tree.map(lambda _: VM, outs),
        compiler_params=pltpu.CompilerParams(vmem_limit_bytes=mib << 20),
        **more,
    )


def query_body(q_ref, lse_ref, out_ref, wide):
    heads, width, rows = q_ref.shape
    row = lax.broadcasted_iota(jnp.int32, (640 - width, rows), 0)
    for h in range(heads):
        value = lse_ref[h : h + 1, :] * (-1.0 / attn_scale)
        p0 = value.astype(bf16).astype(f32)
        p1 = (value - p0).astype(bf16).astype(f32)
        p2 = value - p0 - p1
        more = jnp.where(row == 0, p0, jnp.where(row == 1, p1, jnp.where(row == 2, p2, 0.0)))
        wide[h, 0:width, :] = q_ref[h]
        wide[h, width:, :] = more.astype(bf16)
        out_ref[h] = wide[h].T


def wide_queries(query, normalizer):
    heads, _, rows = query.shape
    return call(
        query_body,
        sds((heads, rows, 640), bf16),
        [VM, VM],
        12,
        scratch_shapes=[pltpu.VMEM((heads, 640, rows), bf16)],
        name="wide_queries",
    )(query, normalizer)


def score_body(q_ref, *refs):
    tiles, before, (out_ref, index_ref, keys) = refs[:8], refs[8:-3], refs[-3:]
    heads, rows, depth = q_ref.shape
    width = tiles[0].shape[0] - 128
    begin = 512 * len(before)
    if before:
        out_ref[:, 0:begin] = before[0][...]
        index_ref[0:begin] = before[1][...]
    for i, tile in enumerate(tiles):
        index_ref[begin + i * 128 : begin + i * 128 + 128] = tile[0:128, :]
    row = lax.broadcasted_iota(jnp.int32, (depth - width, 512), 0)
    for n in range(2):
        keys[n, width:, :] = jnp.where(row < 3, 1.0, 0.0).astype(bf16)
        for i in range(4):
            keys[n, 0:width, i * 128 : i * 128 + 128] = tiles[4 * n + i][128:, :]
        total = None
        for h in range(0, heads, 2):
            both = q_ref[h : h + 2].reshape(2 * rows, depth)
            s = jnp.dot(both, keys[n], preferred_element_type=f32)
            p = jnp.exp2(s * (attn_scale * LOG2E))
            p = p[:rows] + p[rows:]
            total = p if total is None else total + p
        for x in range(4):
            for zh in range(4):
                to, at = (x * 4 + zh) * 16, (zh * 4 + x) * 16
                out_ref[to : to + 16, begin + n * 512 : begin + n * 512 + 512] = total[
                    at : at + 16
                ].astype(bf16)


def scores(query, tiles, *before):
    _, rows, depth = query.shape
    cols = 1024 + 512 * len(before)
    return call(
        score_body,
        (sds((rows, cols), bf16), sds((cols, 128), bf16)),
        [VM] * (9 + len(before)),
        14,
        scratch_shapes=[pltpu.VMEM((2, depth, 512), bf16)],
        name="scores",
    )(query, *tiles, *before)


def weight_column(q_ref, j):
    row = jnp.sum(q_ref[j, 64:80, :].astype(f32), axis=0, keepdims=True)[:, 0:64]
    eye = lax.broadcasted_iota(jnp.int32, (64, 64), 0) == lax.broadcasted_iota(jnp.int32, (64, 64), 1)
    return jnp.sum(jnp.where(eye, row, 0.0), axis=1, keepdims=True)


def slot_tile(at_ref, slot):
    u, k, v = slot // 8, slot // 2 % 4, slot % 2
    y = lax.rem(at_ref[1] + ((0,) + STEPS)[k], 4)
    z = at_ref[2] if u == 0 else 1 - at_ref[2]
    c = at_ref[3] if v == 0 else 1 - at_ref[3]
    return y * 4 + z * 2 + c


def allowed(at_ref, kept_ref):
    half = jnp.where(at_ref[0] >= 8, 1, 0)
    flags = [
        jnp.full((16, 128), kept_ref[half, slot_tile(at_ref, slot)], jnp.int32) for slot in range(16)
    ]
    return jnp.concatenate(flags, axis=1) > 0


NT = (((1,), (1,)), ((), ()))
TN = (((0,), (0,)), ((), ()))


def index_body(scale, at_ref, kept_ref, q_ref, keys, prob_ref, acc):
    acc[...] = jnp.zeros_like(acc)

    @pl.loop(0, 4)
    def _(g):
        rows = q_ref[pl.ds(4 * g, 4), 0:64, :].reshape(256, 128)
        z = lax.dot_general(rows, keys[...], NT, preferred_element_type=f32)
        part = None
        for a in range(4):
            weight = weight_column(q_ref, 4 * g + a) * scale
            term = jnp.maximum(z[a * 64 : a * 64 + 64], 0.0) * weight
            part = term if part is None else part + term
        acc[...] += part

    pick = (
        lax.broadcasted_iota(jnp.int32, (16, 64), 1) // 4
        == lax.broadcasted_iota(jnp.int32, (16, 64), 0)
    ).astype(f32)
    logit = jnp.dot(pick, acc[...], precision=lax.Precision.HIGHEST, preferred_element_type=f32)
    keep = allowed(at_ref, kept_ref)
    top = jnp.max(jnp.where(keep, logit, -jnp.inf), axis=1, keepdims=True)
    expo = jnp.where(keep, jnp.exp(jnp.where(keep, logit, top) - top), 0.0)
    prob_ref[...] = expo / jnp.sum(expo, axis=1, keepdims=True)


def index_forward(at, kept, queries, keys, scale):
    return call(
        functools.partial(index_body, scale),
        sds((16, 2048), f32),
        [SM, SM, VM, VM],
        14,
        scratch_shapes=[pltpu.VMEM((64, 2048), f32)],
        name="index_forward",
    )(at, kept, queries, keys)


def back_body(scale, at_ref, kept_ref, prob_ref, q_ref, keys, sums, *refs):
    own_ref, send_ref, dq_ref, dz, dk, wide = refs
    total = sums[0].astype(f32)
    for j in range(1, sums.shape[0]):
        total += sums[j].astype(f32)
    head_sum = jnp.where(allowed(at_ref, kept_ref), total, 0.0)
    grad = prob_ref[...] - head_sum / jnp.sum(head_sum, axis=1, keepdims=True)
    for t in range(16):
        wide[4 * t : 4 * t + 4, :] = jnp.broadcast_to(grad[t : t + 1], (4, 2048))
    dk[...] = jnp.zeros_like(dk)

    @pl.loop(0, 4)
    def _(g):
        rows = q_ref[pl.ds(4 * g, 4), 0:64, :].reshape(256, 128)
        z = lax.dot_general(rows, keys[...], NT, preferred_element_type=f32)
        for a in range(4):
            at = a * 64
            value = wide[...] * weight_column(q_ref, 4 * g + a)
            dz[at : at + 64, :] = jnp.where(z[at : at + 64] > 0.0, value, 0.0).astype(bf16)
        dk[...] += lax.dot_general(rows, dz[...], TN, preferred_element_type=f32)
        dq = jnp.dot(dz[...], keys[...], preferred_element_type=f32) * scale
        dq_ref[pl.ds(4 * g, 4)] = dq.astype(bf16).reshape(4, 64, 128)

    for slot in range(16):
        tile = dk[:, slot * 128 : slot * 128 + 128] * scale
        place = lax.div(slot_tile(at_ref, slot), 2)
        if slot % 2 == 0:
            own_ref[place] = tile
        else:
            send_ref[place] = tile.astype(bf16)


def index_backward(at, kept, prob, queries, keys, sums, scale):
    return call(
        functools.partial(back_body, scale),
        (sds((8, 128, 128), f32), sds((8, 128, 128), bf16), sds((16, 64, 128), bf16)),
        [SM, SM] + [VM] * 4,
        16,
        scratch_shapes=[
            pltpu.VMEM((256, 2048), bf16),
            pltpu.VMEM((128, 2048), f32),
            pltpu.VMEM((64, 2048), f32),
        ],
        name="index_backward",
    )(at, kept, prob, queries, keys, sums)


def local(query_latent, key_latent, normalizer, index_query, index_key, index_weight, kept):
    index_scale = index_query.shape[2] ** (-0.5)
    head = lax.axis_index("head")
    seq = lax.axis_index("seq")
    at = jnp.stack([head, seq // 4, seq // 2 % 2, seq % 2]).astype(jnp.int32)

    tile = jnp.concatenate([index_key, key_latent.T], axis=0)
    tiles = []
    for u in range(2):
        if u == 1:
            tile = along_z(tile)
        for d in (0,) + STEPS:
            there = along_y(tile, -d) if d else tile
            tiles += [there, other_core(there)]

    w0 = lax.reduce_precision(index_weight, 8, 7)
    w1 = lax.reduce_precision(index_weight - w0, 8, 7)
    w2 = index_weight - w0 - w1
    weight = jnp.stack([w.reshape(16, 64) for w in (w0, w1, w2)], axis=1).astype(bf16)
    weight = jnp.pad(weight, ((0, 0), (0, 13), (0, 64)))
    queries = jnp.concatenate([index_query.reshape(16, 64, 128), weight], axis=1)
    queries = exchanged(queries, "head")

    query = wide_queries(jnp.transpose(query_latent, (1, 2, 0)), normalizer.T)
    first = scores(query, tiles[:8])
    part, index_keys = scores(query, tiles[8:], *first)
    part = exchanged(part.reshape(4, 64, 2048), "head", ROW_X)
    part = jnp.sum(part.astype(f32), axis=0).astype(bf16)
    sums = exchanged(part.reshape(4, 16, 2048), "head", ROW_ZH)

    prob = index_forward(at, kept, queries, index_keys, index_scale)
    own, send, dq = index_backward(at, kept, prob, queries, index_keys, sums, index_scale)

    got = other_core(send)
    dkey = (own + got.astype(f32)).astype(bf16)
    dkey = exchanged(dkey.reshape(32, 32, 128), ("seq", "head"), YZX)
    dkey = jnp.sum(dkey.astype(f32), axis=0).astype(bf16)
    dkey = jnp.broadcast_to(dkey, (16, 32, 128))
    both = exchanged(jnp.concatenate([dq, dkey], axis=1), "head")
    dkey = both[:, 64:].astype(f32).reshape(4, 4, 32, 128).sum(axis=0).reshape(128, 128).T
    return both[:, :64].reshape(index_query.shape), dkey


def solution(mesh):
    return jax.shard_map(
        local,
        mesh=mesh,
        in_specs=(
            P("seq", "head", None),
            P("seq", None),
            P("seq", "head"),
            P("seq", "head", None),
            P("seq", None),
            P("seq", "head"),
            P("seq", None),
        ),
        out_specs=(P("seq", "head", None), P("seq", None)),
        check_vma=False,
    )
```

```python
import functools

import jax
import jax.numpy as jnp
from jax import lax
from jax.experimental import pallas as pl
from jax.experimental.pallas import tpu as pltpu
from jax.sharding import PartitionSpec as P


attn_scale = 192.0 ** (-0.5)
LOG2E = 1.4426950408889634
STEPS = (1, 3, 2)
f32 = jnp.float32
bf16 = jnp.bfloat16
VM = pl.BlockSpec(memory_space=pltpu.VMEM)
SM = pl.BlockSpec(memory_space=pltpu.SMEM)
HB = pl.BlockSpec(memory_space=pltpu.HBM)

ROW_X = [[zh * 4 + x for x in range(4)] for zh in range(4)]
ROW_ZH = [[zh * 4 + x for zh in range(4)] for x in range(4)]
YZX = [
    [(y * 4 + z * 2 + c) * 16 + zh * 4 + x for y in range(4) for z in range(2) for x in range(4)]
    for zh in range(4)
    for c in range(2)
]


def along_y(value, d):
    return lax.ppermute(value, "seq", [(i, (i + 4 * d) % 16) for i in range(16)])


def along_z(value):
    return lax.ppermute(value, "seq", [(i, i ^ 2) for i in range(16)])


def other_core(value):
    return lax.ppermute(value, "seq", [(i, i ^ 1) for i in range(16)])


def along_x(value, d):
    return lax.ppermute(value, "head", [(i, i // 4 * 4 + (i + d) % 4) for i in range(16)])


def along_zh(value, d):
    return lax.ppermute(value, "head", [(i, (i + 4 * d) % 16) for i in range(16)])


def exchanged(value, axis, groups=None):
    return lax.all_to_all(value, axis, 0, 0, tiled=True, axis_index_groups=groups)


def sds(shape, dtype):
    return jax.ShapeDtypeStruct(shape, dtype)


def call(body, outs, specs, mib, out_specs=None, **more):
    return pl.pallas_call(
        body,
        out_shape=outs,
        in_specs=specs,
        out_specs=out_specs or jax.tree.map(lambda _: VM, outs),
        compiler_params=pltpu.CompilerParams(vmem_limit_bytes=mib << 20),
        **more,
    )


def query_body(q_ref, lse_ref, out_ref, wide, turned, in_sem, out_sem):
    heads, width, rows = q_ref.shape
    loads = [
        pltpu.make_async_copy(q_ref.at[h], wide.at[h, 0:width, :], in_sem.at[h]) for h in range(heads)
    ]
    for load in loads:
        load.start()
    row = lax.broadcasted_iota(jnp.int32, (640 - width, rows), 0)
    stores = []
    for h in range(heads):
        value = lse_ref[h : h + 1, :] * (-1.0 / attn_scale)
        p0 = value.astype(bf16).astype(f32)
        p1 = (value - p0).astype(bf16).astype(f32)
        p2 = value - p0 - p1
        more = jnp.where(row == 0, p0, jnp.where(row == 1, p1, jnp.where(row == 2, p2, 0.0)))
        wide[h, width:, :] = more.astype(bf16)
        loads[h].wait()
        flat = wide[h].T
        for x in range(4):
            for zh in range(4):
                at = (zh * 4 + x) * 16
                turned[h, x, zh * 16 : zh * 16 + 16, :] = flat[at : at + 16]
        stores.append(pltpu.make_async_copy(turned.at[h], out_ref.at[:, h], out_sem.at[h]))
        stores[-1].start()
    for store in stores:
        store.wait()


def wide_queries(query, normalizer):
    heads, _, rows = query.shape
    return call(
        query_body,
        pltpu.HBM((4, heads, rows // 4, 640), bf16),
        [HB, VM],
        12,
        out_specs=HB,
        scratch_shapes=[
            pltpu.VMEM((heads, 640, rows), bf16),
            pltpu.VMEM((heads, 4, rows // 4, 640), bf16),
            pltpu.SemaphoreType.DMA((heads,)),
            pltpu.SemaphoreType.DMA((heads,)),
        ],
        name="wide_queries",
    )(pltpu.with_memory_space_constraint(query, pltpu.HBM), normalizer)


def score_body(q_hbm, *refs):
    tiles, (out_ref, index_ref, q_ref, keys, q_sem, k_sem, i_sem) = refs[:16], refs[16:]
    groups, heads, rows, depth = q_ref.shape
    width = tiles[0].shape[0] - 128
    key_loads, index_loads = [], []
    for i, tile in enumerate(tiles):
        place = keys.at[i // 4, 0:width, i % 4 * 128 : i % 4 * 128 + 128]
        key_loads.append(pltpu.make_async_copy(tile.at[128 : 128 + width, :], place, k_sem.at[i]))
        place = index_ref.at[i * 128 : i * 128 + 128, :]
        index_loads.append(pltpu.make_async_copy(tile.at[0:128, :], place, i_sem.at[i]))
    q_loads = [
        pltpu.make_async_copy(q_hbm.at[a], q_ref.at[a], q_sem.at[a]) for a in range(groups)
    ]
    for load in q_loads[:1] + key_loads[:4] + q_loads[1:] + key_loads[4:] + index_loads:
        load.start()
    row = lax.broadcasted_iota(jnp.int32, (depth - width, 512), 0)
    for n in range(4):
        keys[n, width:, :] = jnp.where(row < 3, 1.0, 0.0).astype(bf16)
        for load in key_loads[4 * n : 4 * n + 4]:
            load.wait()
        total = None
        for a in range(groups):
            if n == 0:
                q_loads[a].wait()
            some = q_ref[a].reshape(heads * rows, depth)
            s = jnp.dot(some, keys[n], preferred_element_type=f32)
            p = jnp.exp2(s * (attn_scale * LOG2E))
            for h in range(heads):
                part = p[h * rows : h * rows + rows]
                total = part if total is None else total + part
        out_ref[:, n * 512 : n * 512 + 512] = total.astype(bf16)
    for load in index_loads:
        load.wait()


def scores(query, tiles):
    groups, _, rows, depth = query.shape
    return call(
        score_body,
        (sds((rows, 2048), bf16), sds((2048, 128), bf16)),
        [HB] * 17,
        16,
        scratch_shapes=[
            pltpu.VMEM(query.shape, bf16),
            pltpu.VMEM((4, depth, 512), bf16),
            pltpu.SemaphoreType.DMA((groups,)),
            pltpu.SemaphoreType.DMA((16,)),
            pltpu.SemaphoreType.DMA((16,)),
        ],
        name="scores",
    )(*[pltpu.with_memory_space_constraint(v, pltpu.HBM) for v in (query, *tiles)])


def pack_body(at_ref, q_ref, w_ref, *outs):
    for d, ref in zip((0,) + STEPS, outs):
        x = lax.rem(at_ref[1] + d, 4)
        for zh in range(4):
            ref[zh, 0:64, :] = q_ref[zh * 4 + x]
            ref[zh, 64:80, :] = w_ref[zh * 4 + x]


def spread_body(at_ref, *refs):
    for d, ref in zip((0,) + STEPS, refs[4:]):
        zh = lax.rem(at_ref[0] + d, 4)
        for a in range(4):
            ref[a] = refs[a][zh]


def weight_column(q_ref, j):
    row = jnp.sum(q_ref[j, 64:80, :].astype(f32), axis=0, keepdims=True)[:, 0:64]
    eye = lax.broadcasted_iota(jnp.int32, (64, 64), 0) == lax.broadcasted_iota(jnp.int32, (64, 64), 1)
    return jnp.sum(jnp.where(eye, row, 0.0), axis=1, keepdims=True)


def slot_tile(at_ref, slot):
    u, k, v = slot // 8, slot // 2 % 4, slot % 2
    y = lax.rem(at_ref[2] + ((0,) + STEPS)[k], 4)
    z = at_ref[3] if u == 0 else 1 - at_ref[3]
    c = at_ref[4] if v == 0 else 1 - at_ref[4]
    return y * 4 + z * 2 + c


def allowed(at_ref, kept_ref):
    half = jnp.where(at_ref[0] >= 2, 1, 0)
    flags = [
        jnp.full((16, 128), kept_ref[half, slot_tile(at_ref, slot)], jnp.int32) for slot in range(16)
    ]
    return jnp.concatenate(flags, axis=1) > 0


NT = (((1,), (1,)), ((), ()))
TN = (((0,), (0,)), ((), ()))


def index_body(scale, at_ref, kept_ref, *refs):
    keys, prob_ref, q_ref, acc = refs[4:]
    for g in range(4):
        for a in range(4):
            q_ref[4 * g + a] = refs[g][a]
    acc[...] = jnp.zeros_like(acc)

    @pl.loop(0, 4)
    def _(g):
        rows = q_ref[pl.ds(4 * g, 4), 0:64, :].reshape(256, 128)
        z = lax.dot_general(rows, keys[...], NT, preferred_element_type=f32)
        part = None
        for a in range(4):
            weight = weight_column(q_ref, 4 * g + a) * scale
            term = jnp.maximum(z[a * 64 : a * 64 + 64], 0.0) * weight
            part = term if part is None else part + term
        acc[...] += part

    pick = (
        lax.broadcasted_iota(jnp.int32, (16, 64), 1) // 4
        == lax.broadcasted_iota(jnp.int32, (16, 64), 0)
    ).astype(f32)
    logit = jnp.dot(pick, acc[...], precision=lax.Precision.HIGHEST, preferred_element_type=f32)
    keep = allowed(at_ref, kept_ref)
    top = jnp.max(jnp.where(keep, logit, -jnp.inf), axis=1, keepdims=True)
    expo = jnp.where(keep, jnp.exp(jnp.where(keep, logit, top) - top), 0.0)
    prob_ref[...] = expo / jnp.sum(expo, axis=1, keepdims=True)


def index_forward(at, kept, queries, keys, scale):
    return call(
        functools.partial(index_body, scale),
        (sds((16, 2048), f32), sds((16, 80, 128), bf16)),
        [SM, SM] + [VM] * 5,
        14,
        scratch_shapes=[pltpu.VMEM((64, 2048), f32)],
        name="index_forward",
    )(at, kept, *queries, keys)


def back_body(scale, at_ref, kept_ref, prob_ref, q_ref, keys, sums, *refs):
    own_ref, send_ref, dq_ref, dz, dk, wide = refs
    total = sums[0].astype(f32)
    for j in range(1, sums.shape[0]):
        total += sums[j].astype(f32)
    head_sum = jnp.where(allowed(at_ref, kept_ref), total, 0.0)
    grad = prob_ref[...] - head_sum / jnp.sum(head_sum, axis=1, keepdims=True)
    for t in range(16):
        wide[4 * t : 4 * t + 4, :] = jnp.broadcast_to(grad[t : t + 1], (4, 2048))
    dk[...] = jnp.zeros_like(dk)

    @pl.loop(0, 4)
    def _(g):
        rows = q_ref[pl.ds(4 * g, 4), 0:64, :].reshape(256, 128)
        z = lax.dot_general(rows, keys[...], NT, preferred_element_type=f32)
        for a in range(4):
            at = a * 64
            value = wide[...] * weight_column(q_ref, 4 * g + a)
            dz[at : at + 64, :] = jnp.where(z[at : at + 64] > 0.0, value, 0.0).astype(bf16)
        dk[...] += lax.dot_general(rows, dz[...], TN, preferred_element_type=f32)
        dq = jnp.dot(dz[...], keys[...], preferred_element_type=f32) * scale
        e = jnp.where(g < 2, g, 5 - g)
        zh = lax.rem(at_ref[0] + 4 - e, 4)
        for a, d in enumerate((0,) + STEPS):
            x = lax.rem(at_ref[1] + 4 - d, 4)
            dq_ref[zh * 4 + x] = dq[a * 64 : a * 64 + 64].astype(bf16)

    for slot in range(16):
        tile = dk[:, slot * 128 : slot * 128 + 128] * scale
        place = lax.div(slot_tile(at_ref, slot), 2)
        if slot % 2 == 0:
            own_ref[place] = tile
        else:
            send_ref[place] = tile.astype(bf16)


def index_backward(at, kept, prob, queries, keys, sums, scale):
    return call(
        functools.partial(back_body, scale),
        (sds((8, 128, 128), f32), sds((8, 128, 128), bf16), sds((16, 64, 128), bf16)),
        [SM, SM] + [VM] * 4,
        16,
        scratch_shapes=[
            pltpu.VMEM((256, 2048), bf16),
            pltpu.VMEM((128, 2048), f32),
            pltpu.VMEM((64, 2048), f32),
        ],
        name="index_backward",
    )(at, kept, prob, queries, keys, sums)


def local(query_latent, key_latent, normalizer, index_query, index_key, index_weight, kept):
    index_scale = index_query.shape[2] ** (-0.5)
    head = lax.axis_index("head")
    seq = lax.axis_index("seq")
    at = jnp.stack([head // 4, head % 4, seq // 4, seq // 2 % 2, seq % 2]).astype(jnp.int32)

    tile = jnp.concatenate([index_key, key_latent.T], axis=0)
    tiles = []
    for u in range(2):
        if u == 1:
            tile = along_z(tile)
        for d in (0,) + STEPS:
            there = along_y(tile, -d) if d else tile
            tiles += [there, other_core(there)]

    w0 = lax.reduce_precision(index_weight, 8, 7)
    w1 = lax.reduce_precision(index_weight - w0, 8, 7)
    w2 = index_weight - w0 - w1
    weight = jnp.stack([w.reshape(16, 64) for w in (w0, w1, w2)], axis=1).astype(bf16)
    weight = jnp.pad(weight, ((0, 0), (0, 13), (0, 64)))
    four = (sds((4, 80, 128), bf16),) * 4
    parts = call(pack_body, four, [SM, VM, VM], 6, name="pack")(
        at, index_query.reshape(16, 64, 128), weight
    )
    got = [parts[0]]
    for part, d in zip(parts[1:], STEPS):
        got.append(along_x(part, d))
    parts = call(spread_body, four, [SM] + [VM] * 4, 6, name="spread")(at, *got)
    queries = [parts[0]]
    for part, d in zip(parts[1:], STEPS):
        queries.append(along_zh(part, d))

    query = wide_queries(jnp.transpose(query_latent, (1, 2, 0)), normalizer.T)
    query = exchanged(query, "head", ROW_X)
    part, index_keys = scores(query, tiles)
    sums = exchanged(part.reshape(4, 16, 2048), "head", ROW_ZH)

    prob, queries = index_forward(at, kept, queries, index_keys, index_scale)
    own, send, dq = index_backward(at, kept, prob, queries, index_keys, sums, index_scale)

    got = other_core(send)
    dkey = (own + got.astype(f32)).astype(bf16)
    dkey = exchanged(dkey.reshape(32, 32, 128), ("seq", "head"), YZX)
    dkey = jnp.sum(dkey.astype(f32), axis=0).astype(bf16)
    dkey = jnp.broadcast_to(dkey, (16, 32, 128))
    both = exchanged(jnp.concatenate([dq, dkey], axis=1), "head")
    dkey = both[:, 64:].astype(f32).reshape(4, 4, 32, 128).sum(axis=0).reshape(128, 128).T
    return both[:, :64].reshape(index_query.shape), dkey


def solution(mesh):
    return jax.shard_map(
        local,
        mesh=mesh,
        in_specs=(
            P("seq", "head", None),
            P("seq", None),
            P("seq", "head"),
            P("seq", "head", None),
            P("seq", None),
            P("seq", "head"),
            P("seq", None),
        ),
        out_specs=(P("seq", "head", None), P("seq", None)),
        check_vma=False,
    )
```

```python
import functools

import jax
import jax.numpy as jnp
from jax import lax
from jax.experimental import pallas as pl
from jax.experimental.pallas import tpu as pltpu
from jax.sharding import PartitionSpec as P


attn_scale = 192.0 ** (-0.5)
LOG2E = 1.4426950408889634
STEPS = (1, 3, 2)
f32 = jnp.float32
bf16 = jnp.bfloat16
VM = pl.BlockSpec(memory_space=pltpu.VMEM)
SM = pl.BlockSpec(memory_space=pltpu.SMEM)
HB = pl.BlockSpec(memory_space=pltpu.HBM)

ROW_X = [[zh * 4 + x for x in range(4)] for zh in range(4)]
ROW_ZH = [[zh * 4 + x for zh in range(4)] for x in range(4)]
YZX = [
    [(y * 4 + z * 2 + c) * 16 + zh * 4 + x for y in range(4) for z in range(2) for x in range(4)]
    for zh in range(4)
    for c in range(2)
]


def along_y(value, d):
    return lax.ppermute(value, "seq", [(i, (i + 4 * d) % 16) for i in range(16)])


def along_z(value):
    return lax.ppermute(value, "seq", [(i, i ^ 2) for i in range(16)])


def other_core(value):
    return lax.ppermute(value, "seq", [(i, i ^ 1) for i in range(16)])


def along_x(value, d):
    return lax.ppermute(value, "head", [(i, i // 4 * 4 + (i + d) % 4) for i in range(16)])


def along_zh(value, d):
    return lax.ppermute(value, "head", [(i, (i + 4 * d) % 16) for i in range(16)])


def exchanged(value, axis, groups=None):
    return lax.all_to_all(value, axis, 0, 0, tiled=True, axis_index_groups=groups)


def sds(shape, dtype):
    return jax.ShapeDtypeStruct(shape, dtype)


def call(body, outs, specs, mib, out_specs=None, **more):
    return pl.pallas_call(
        body,
        out_shape=outs,
        in_specs=specs,
        out_specs=out_specs or jax.tree.map(lambda _: VM, outs),
        compiler_params=pltpu.CompilerParams(vmem_limit_bytes=mib << 20),
        **more,
    )


def query_body(q_ref, lse_hbm, out_ref, wide, turned, lse_ref, in_sem, out_sem):
    heads, width, rows = q_ref.shape
    loads = [
        pltpu.make_async_copy(q_ref.at[h], wide.at[h, 0:width, :], in_sem.at[h]) for h in range(heads)
    ]
    lse_load = pltpu.make_async_copy(lse_hbm, lse_ref, in_sem.at[heads])
    for load in [lse_load] + loads:
        load.start()
    row = lax.broadcasted_iota(jnp.int32, (640 - width, rows), 0)
    lse_load.wait()
    stores = []
    for h in range(heads):
        value = lse_ref[h : h + 1, :] * (-1.0 / attn_scale)
        p0 = value.astype(bf16).astype(f32)
        p1 = (value - p0).astype(bf16).astype(f32)
        p2 = value - p0 - p1
        more = jnp.where(row == 0, p0, jnp.where(row == 1, p1, jnp.where(row == 2, p2, 0.0)))
        wide[h, width:, :] = more.astype(bf16)
        loads[h].wait()
        flat = wide[h].T
        for x in range(4):
            for zh in range(4):
                at = (zh * 4 + x) * 16
                turned[h, x, zh * 16 : zh * 16 + 16, :] = flat[at : at + 16]
        stores.append(pltpu.make_async_copy(turned.at[h], out_ref.at[:, h], out_sem.at[h]))
        stores[-1].start()
    for store in stores:
        store.wait()


def wide_queries(query, normalizer):
    heads, _, rows = query.shape
    return call(
        query_body,
        pltpu.HBM((4, heads, rows // 4, 640), bf16),
        [HB, HB],
        12,
        out_specs=HB,
        scratch_shapes=[
            pltpu.VMEM((heads, 640, rows), bf16),
            pltpu.VMEM((heads, 4, rows // 4, 640), bf16),
            pltpu.VMEM((heads, rows), f32),
            pltpu.SemaphoreType.DMA((heads + 1,)),
            pltpu.SemaphoreType.DMA((heads,)),
        ],
        name="wide_queries",
    )(*[pltpu.with_memory_space_constraint(v, pltpu.HBM) for v in (query, normalizer)])


def score_body(q_hbm, *refs):
    tiles, (out_ref, index_ref, q_ref, keys, acc, q_sem) = refs[:16], refs[16:]
    groups, heads, rows, depth = q_ref.shape
    width = tiles[0].shape[0] - 128
    q_loads = [
        pltpu.make_async_copy(q_hbm.at[a], q_ref.at[a], q_sem.at[a]) for a in range(groups)
    ]
    for load in q_loads:
        load.start()
    row = lax.broadcasted_iota(jnp.int32, (depth - width, 512), 0)
    for n in range(4):
        keys[n, width:, :] = jnp.where(row < 3, 1.0, 0.0).astype(bf16)
    for i, tile in enumerate(tiles):
        keys[i // 4, 0:width, i % 4 * 128 : i % 4 * 128 + 128] = tile[128 : 128 + width, :]
        index_ref[i * 128 : i * 128 + 128, :] = tile[0:128, :]
    for a in range(groups):
        q_loads[a].wait()
        some = q_ref[a].reshape(heads * rows, depth)
        for n in range(4):
            at = n * 512
            s = jnp.dot(some, keys[n], preferred_element_type=f32)
            p = jnp.exp2(s * (attn_scale * LOG2E))
            total = acc[:, at : at + 512] if a else None
            for h in range(heads):
                part = p[h * rows : h * rows + rows]
                total = part if total is None else total + part
            if a + 1 < groups:
                acc[:, at : at + 512] = total
            else:
                out_ref[:, at : at + 512] = total.astype(bf16)


def scores(query, tiles):
    groups, _, rows, depth = query.shape
    return call(
        score_body,
        (sds((rows, 2048), bf16), sds((2048, 128), bf16)),
        [HB] + [VM] * 16,
        16,
        scratch_shapes=[
            pltpu.VMEM(query.shape, bf16),
            pltpu.VMEM((4, depth, 512), bf16),
            pltpu.VMEM((rows, 2048), f32),
            pltpu.SemaphoreType.DMA((groups,)),
        ],
        name="scores",
    )(pltpu.with_memory_space_constraint(query, pltpu.HBM), *tiles)


def pack_body(at_ref, q_ref, w_ref, *outs):
    for d, ref in zip((0,) + STEPS, outs):
        zh = lax.rem(at_ref[0] + d, 4)
        for x in range(4):
            ref[x, 0:64, :] = q_ref[zh * 4 + x]
            ref[x, 64:80, :] = w_ref[zh * 4 + x]


def spread_body(at_ref, *refs):
    for d, ref in zip((0,) + STEPS, refs[4:]):
        x = lax.rem(at_ref[1] + d, 4)
        for e in range(4):
            ref[e] = refs[e][x]


def weight_column(q_ref, j):
    row = jnp.sum(q_ref[j, 64:80, :].astype(f32), axis=0, keepdims=True)[:, 0:64]
    eye = lax.broadcasted_iota(jnp.int32, (64, 64), 0) == lax.broadcasted_iota(jnp.int32, (64, 64), 1)
    return jnp.sum(jnp.where(eye, row, 0.0), axis=1, keepdims=True)


def slot_tile(at_ref, slot):
    u, k, v = slot // 8, slot // 2 % 4, slot % 2
    y = lax.rem(at_ref[2] + ((0,) + STEPS)[k], 4)
    z = at_ref[3] if u == 0 else 1 - at_ref[3]
    c = at_ref[4] if v == 0 else 1 - at_ref[4]
    return y * 4 + z * 2 + c


def allowed(at_ref, kept_ref):
    half = jnp.where(at_ref[0] >= 2, 1, 0)
    flags = [
        jnp.full((16, 128), kept_ref[half, slot_tile(at_ref, slot)], jnp.int32) for slot in range(16)
    ]
    return jnp.concatenate(flags, axis=1) > 0


NT = (((1,), (1,)), ((), ()))
TN = (((0,), (0,)), ((), ()))


def index_body(scale, at_ref, kept_ref, *refs):
    keys, prob_ref, q_ref, acc = refs[4:]
    for g in range(4):
        for a in range(4):
            q_ref[4 * g + a] = refs[g][a]
    acc[...] = jnp.zeros_like(acc)

    @pl.loop(0, 4)
    def _(g):
        rows = q_ref[pl.ds(4 * g, 4), 0:64, :].reshape(256, 128)
        z = lax.dot_general(rows, keys[...], NT, preferred_element_type=f32)
        part = None
        for a in range(4):
            weight = weight_column(q_ref, 4 * g + a) * scale
            term = jnp.maximum(z[a * 64 : a * 64 + 64], 0.0) * weight
            part = term if part is None else part + term
        acc[...] += part

    pick = (
        lax.broadcasted_iota(jnp.int32, (16, 64), 1) // 4
        == lax.broadcasted_iota(jnp.int32, (16, 64), 0)
    ).astype(f32)
    logit = jnp.dot(pick, acc[...], precision=lax.Precision.HIGHEST, preferred_element_type=f32)
    keep = allowed(at_ref, kept_ref)
    top = jnp.max(jnp.where(keep, logit, -jnp.inf), axis=1, keepdims=True)
    expo = jnp.where(keep, jnp.exp(jnp.where(keep, logit, top) - top), 0.0)
    prob_ref[...] = expo / jnp.sum(expo, axis=1, keepdims=True)


def index_forward(at, kept, queries, keys, scale):
    return call(
        functools.partial(index_body, scale),
        (sds((16, 2048), f32), sds((16, 80, 128), bf16)),
        [SM, SM] + [VM] * 5,
        14,
        scratch_shapes=[pltpu.VMEM((64, 2048), f32)],
        name="index_forward",
    )(at, kept, *queries, keys)


def back_body(scale, at_ref, kept_ref, prob_ref, q_ref, keys, sums, *refs):
    own_ref, send_ref, dq_ref, dz, dk, wide = refs
    total = sums[0].astype(f32)
    for j in range(1, sums.shape[0]):
        total += sums[j].astype(f32)
    head_sum = jnp.where(allowed(at_ref, kept_ref), total, 0.0)
    grad = prob_ref[...] - head_sum / jnp.sum(head_sum, axis=1, keepdims=True)
    for t in range(16):
        wide[4 * t : 4 * t + 4, :] = jnp.broadcast_to(grad[t : t + 1], (4, 2048))
    dk[...] = jnp.zeros_like(dk)

    @pl.loop(0, 4)
    def _(g):
        rows = q_ref[pl.ds(4 * g, 4), 0:64, :].reshape(256, 128)
        z = lax.dot_general(rows, keys[...], NT, preferred_element_type=f32)
        for a in range(4):
            at = a * 64
            value = wide[...] * weight_column(q_ref, 4 * g + a)
            dz[at : at + 64, :] = jnp.where(z[at : at + 64] > 0.0, value, 0.0).astype(bf16)
        dk[...] += lax.dot_general(rows, dz[...], TN, preferred_element_type=f32)
        dq = jnp.dot(dz[...], keys[...], preferred_element_type=f32) * scale
        d = jnp.where(g < 2, g, 5 - g)
        x = lax.rem(at_ref[1] + 4 - d, 4)
        for a, e in enumerate((0,) + STEPS):
            zh = lax.rem(at_ref[0] + 4 - e, 4)
            dq_ref[zh * 4 + x] = dq[a * 64 : a * 64 + 64].astype(bf16)

    for slot in range(16):
        tile = dk[:, slot * 128 : slot * 128 + 128] * scale
        place = lax.div(slot_tile(at_ref, slot), 2)
        if slot % 2 == 0:
            own_ref[place] = tile
        else:
            send_ref[place] = tile.astype(bf16)


def index_backward(at, kept, prob, queries, keys, sums, scale):
    return call(
        functools.partial(back_body, scale),
        (sds((8, 128, 128), f32), sds((8, 128, 128), bf16), sds((16, 64, 128), bf16)),
        [SM, SM] + [VM] * 4,
        16,
        scratch_shapes=[
            pltpu.VMEM((256, 2048), bf16),
            pltpu.VMEM((128, 2048), f32),
            pltpu.VMEM((64, 2048), f32),
        ],
        name="index_backward",
    )(at, kept, prob, queries, keys, sums)


def local(query_latent, key_latent, normalizer, index_query, index_key, index_weight, kept):
    index_scale = index_query.shape[2] ** (-0.5)
    head = lax.axis_index("head")
    seq = lax.axis_index("seq")
    at = jnp.stack([head // 4, head % 4, seq // 4, seq // 2 % 2, seq % 2]).astype(jnp.int32)

    tile = jnp.concatenate([index_key, key_latent.T], axis=0)
    tiles = []
    for u in range(2):
        if u == 1:
            tile = along_z(tile)
        for d in (0,) + STEPS:
            there = along_y(tile, -d) if d else tile
            tiles += [there, other_core(there)]

    w0 = lax.reduce_precision(index_weight, 8, 7)
    w1 = lax.reduce_precision(index_weight - w0, 8, 7)
    w2 = index_weight - w0 - w1
    weight = jnp.stack([w.reshape(16, 64) for w in (w0, w1, w2)], axis=1).astype(bf16)
    weight = jnp.pad(weight, ((0, 0), (0, 13), (0, 64)))
    four = (sds((4, 80, 128), bf16),) * 4
    parts = call(pack_body, four, [SM, VM, VM], 6, name="pack")(
        at, index_query.reshape(16, 64, 128), weight
    )
    got = [parts[0]]
    for part, d in zip(parts[1:], STEPS):
        got.append(along_zh(part, d))
    parts = call(spread_body, four, [SM] + [VM] * 4, 6, name="spread")(at, *got)
    queries = [parts[0]]
    for part, d in zip(parts[1:], STEPS):
        queries.append(along_x(part, d))

    query = wide_queries(jnp.transpose(query_latent, (1, 2, 0)), normalizer.T)
    query = exchanged(query, "head", ROW_X)
    part, index_keys = scores(query, tiles)
    sums = exchanged(part.reshape(4, 16, 2048), "head", ROW_ZH)

    prob, queries = index_forward(at, kept, queries, index_keys, index_scale)
    own, send, dq = index_backward(at, kept, prob, queries, index_keys, sums, index_scale)

    got = other_core(send)
    dkey = (own + got.astype(f32)).astype(bf16)
    dkey = exchanged(dkey.reshape(32, 32, 128), ("seq", "head"), YZX)
    dkey = jnp.sum(dkey.astype(f32), axis=0).astype(bf16)
    dkey = jnp.broadcast_to(dkey, (16, 32, 128))
    both = exchanged(jnp.concatenate([dq, dkey], axis=1), "head")
    dkey = both[:, 64:].astype(f32).reshape(4, 4, 32, 128).sum(axis=0).reshape(128, 128).T
    return both[:, :64].reshape(index_query.shape), dkey


def solution(mesh):
    return jax.shard_map(
        local,
        mesh=mesh,
        in_specs=(
            P("seq", "head", None),
            P("seq", None),
            P("seq", "head"),
            P("seq", "head", None),
            P("seq", None),
            P("seq", "head"),
            P("seq", None),
        ),
        out_specs=(P("seq", "head", None), P("seq", None)),
        check_vma=False,
    )
```

```python
import functools

import jax
import jax.numpy as jnp
from jax import lax
from jax.experimental import pallas as pl
from jax.experimental.pallas import tpu as pltpu
from jax.sharding import PartitionSpec as P


attn_scale = 192.0 ** (-0.5)
LOG2E = 1.4426950408889634
STEPS = (1, 3, 2)
f32 = jnp.float32
bf16 = jnp.bfloat16
VM = pl.BlockSpec(memory_space=pltpu.VMEM)
SM = pl.BlockSpec(memory_space=pltpu.SMEM)
HB = pl.BlockSpec(memory_space=pltpu.HBM)

ROW_ZH = [[zh * 4 + x for zh in range(4)] for x in range(4)]
YZX = [
    [(y * 4 + z * 2 + c) * 16 + zh * 4 + x for y in range(4) for z in range(2) for x in range(4)]
    for zh in range(4)
    for c in range(2)
]


def along_y(value, d):
    return lax.ppermute(value, "seq", [(i, (i + 4 * d) % 16) for i in range(16)])


def along_z(value):
    return lax.ppermute(value, "seq", [(i, i ^ 2) for i in range(16)])


def other_core(value):
    return lax.ppermute(value, "seq", [(i, i ^ 1) for i in range(16)])


def along_x(value, d):
    return lax.ppermute(value, "head", [(i, i // 4 * 4 + (i + d) % 4) for i in range(16)])


def exchanged(value, axis, groups=None):
    return lax.all_to_all(value, axis, 0, 0, tiled=True, axis_index_groups=groups)


def sds(shape, dtype):
    return jax.ShapeDtypeStruct(shape, dtype)


def call(body, outs, specs, mib, out_specs=None, **more):
    return pl.pallas_call(
        body,
        out_shape=outs,
        in_specs=specs,
        out_specs=out_specs or jax.tree.map(lambda _: VM, outs),
        compiler_params=pltpu.CompilerParams(vmem_limit_bytes=mib << 20),
        **more,
    )


def query_body(at_ref, q_ref, lse_hbm, o0, o1, o2, o3, wide, turned, lse_ref, in_sem, out_sem):
    heads, width, rows = q_ref.shape
    loads = [
        pltpu.make_async_copy(q_ref.at[h], wide.at[h, 0:width, :], in_sem.at[h]) for h in range(heads)
    ]
    lse_load = pltpu.make_async_copy(lse_hbm, lse_ref, in_sem.at[heads])
    for load in [lse_load] + loads:
        load.start()
    row = lax.broadcasted_iota(jnp.int32, (640 - width, rows), 0)
    lse_load.wait()
    stores = []
    for h in range(heads):
        value = lse_ref[h : h + 1, :] * (-1.0 / attn_scale)
        p0 = value.astype(bf16).astype(f32)
        p1 = (value - p0).astype(bf16).astype(f32)
        p2 = value - p0 - p1
        more = jnp.where(row == 0, p0, jnp.where(row == 1, p1, jnp.where(row == 2, p2, 0.0)))
        wide[h, width:, :] = more.astype(bf16)
        loads[h].wait()
        flat = wide[h].T
        for x in range(4):
            for zh in range(4):
                at = (zh * 4 + x) * 16
                turned[h, x, zh * 16 : zh * 16 + 16, :] = flat[at : at + 16]
        for i, out in enumerate((o0, o1, o2, o3)):
            x = lax.rem(at_ref[1] + ((0,) + STEPS)[i], 4)
            store = pltpu.make_async_copy(turned.at[h, x], out.at[h], out_sem.at[4 * h + i])
            store.start()
            stores.append(store)
    for store in stores:
        store.wait()


def in_hbm(*values):
    return [pltpu.with_memory_space_constraint(v, pltpu.HBM) for v in values]


def wide_queries(at, query, normalizer):
    heads, _, rows = query.shape
    return call(
        query_body,
        (pltpu.HBM((heads, rows // 4, 640), bf16),) * 4,
        [SM, HB, HB],
        12,
        out_specs=(HB,) * 4,
        scratch_shapes=[
            pltpu.VMEM((heads, 640, rows), bf16),
            pltpu.VMEM((heads, 4, rows // 4, 640), bf16),
            pltpu.VMEM((heads, rows), f32),
            pltpu.SemaphoreType.DMA((heads + 1,)),
            pltpu.SemaphoreType.DMA((4 * heads,)),
        ],
        name="wide_queries",
    )(at, *in_hbm(query, normalizer))


def score_body(groups, last, *refs):
    q_hbm, tiles, refs = refs[:groups], refs[groups : groups + 16], refs[groups + 16 :]
    before, (out_ref, *index, q_ref, keys, acc, q_sem) = refs[:last], refs[last:]
    heads, rows, depth = q_ref.shape[1:]
    width = tiles[0].shape[0] - 128
    q_loads = [
        pltpu.make_async_copy(q_hbm[a], q_ref.at[a], q_sem.at[a]) for a in range(groups)
    ]
    for load in q_loads:
        load.start()
    row = lax.broadcasted_iota(jnp.int32, (depth - width, 512), 0)
    for n in range(4):
        keys[n, width:, :] = jnp.where(row < 3, 1.0, 0.0).astype(bf16)
    for i, tile in enumerate(tiles):
        keys[i // 4, 0:width, i % 4 * 128 : i % 4 * 128 + 128] = tile[128 : 128 + width, :]
        for index_ref in index:
            index_ref[i * 128 : i * 128 + 128, :] = tile[0:128, :]
    for a in range(groups):
        q_loads[a].wait()
        some = q_ref[a].reshape(heads * rows, depth)
        for n in range(4):
            at = n * 512
            s = jnp.dot(some, keys[n], preferred_element_type=f32)
            p = jnp.exp2(s * (attn_scale * LOG2E))
            total = acc[:, at : at + 512] if a else None
            for ref in before if a == 0 else ():
                total = ref[:, at : at + 512]
            for h in range(heads):
                part = p[h * rows : h * rows + rows]
                total = part if total is None else total + part
            if a + 1 < groups:
                acc[:, at : at + 512] = total
            else:
                out_ref[:, at : at + 512] = total.astype(out_ref.dtype)


def scores(queries, tiles, *before):
    heads, rows, depth = queries[0].shape
    groups, last = len(queries), len(before)
    return call(
        functools.partial(score_body, groups, last),
        (sds((rows, 2048), bf16),) if last else (sds((rows, 2048), f32), sds((2048, 128), bf16)),
        [HB] * groups + [VM] * (16 + last),
        16,
        scratch_shapes=[
            pltpu.VMEM((groups, heads, rows, depth), bf16),
            pltpu.VMEM((4, depth, 512), bf16),
            pltpu.VMEM((rows, 2048), f32),
            pltpu.SemaphoreType.DMA((groups,)),
        ],
        name="scores",
    )(*in_hbm(*queries), *tiles, *before)


def weight_column(q_ref, j):
    row = jnp.sum(q_ref[j, 64:80, :].astype(f32), axis=0, keepdims=True)[:, 0:64]
    eye = lax.broadcasted_iota(jnp.int32, (64, 64), 0) == lax.broadcasted_iota(jnp.int32, (64, 64), 1)
    return jnp.sum(jnp.where(eye, row, 0.0), axis=1, keepdims=True)


def slot_tile(at_ref, slot):
    u, k, v = slot // 8, slot // 2 % 4, slot % 2
    y = lax.rem(at_ref[2] + ((0,) + STEPS)[k], 4)
    z = at_ref[3] if u == 0 else 1 - at_ref[3]
    c = at_ref[4] if v == 0 else 1 - at_ref[4]
    return y * 4 + z * 2 + c


def allowed(at_ref, kept_ref):
    half = jnp.where(at_ref[0] >= 2, 1, 0)
    flags = [
        jnp.full((16, 128), kept_ref[half, slot_tile(at_ref, slot)], jnp.int32) for slot in range(16)
    ]
    return jnp.concatenate(flags, axis=1) > 0


NT = (((1,), (1,)), ((), ()))
TN = (((0,), (0,)), ((), ()))


def index_body(scale, at_ref, kept_ref, q_ref, keys, prob_ref, acc):
    acc[...] = jnp.zeros_like(acc)

    @pl.loop(0, 4)
    def _(g):
        rows = q_ref[pl.ds(4 * g, 4), 0:64, :].reshape(256, 128)
        z = lax.dot_general(rows, keys[...], NT, preferred_element_type=f32)
        part = None
        for a in range(4):
            weight = weight_column(q_ref, 4 * g + a) * scale
            term = jnp.maximum(z[a * 64 : a * 64 + 64], 0.0) * weight
            part = term if part is None else part + term
        acc[...] += part

    pick = (
        lax.broadcasted_iota(jnp.int32, (16, 64), 1) // 4
        == lax.broadcasted_iota(jnp.int32, (16, 64), 0)
    ).astype(f32)
    logit = jnp.dot(pick, acc[...], precision=lax.Precision.HIGHEST, preferred_element_type=f32)
    keep = allowed(at_ref, kept_ref)
    top = jnp.max(jnp.where(keep, logit, -jnp.inf), axis=1, keepdims=True)
    expo = jnp.where(keep, jnp.exp(jnp.where(keep, logit, top) - top), 0.0)
    prob_ref[...] = expo / jnp.sum(expo, axis=1, keepdims=True)


def index_forward(at, kept, queries, keys, scale):
    return call(
        functools.partial(index_body, scale),
        sds((16, 2048), f32),
        [SM, SM, VM, VM],
        14,
        scratch_shapes=[pltpu.VMEM((64, 2048), f32)],
        name="index_forward",
    )(at, kept, queries, keys)


def back_body(scale, at_ref, kept_ref, prob_ref, q_ref, keys, sums, *refs):
    own_ref, send_ref, dq_ref, dz, dk, wide = refs
    total = sums[0].astype(f32)
    for j in range(1, sums.shape[0]):
        total += sums[j].astype(f32)
    head_sum = jnp.where(allowed(at_ref, kept_ref), total, 0.0)
    grad = prob_ref[...] - head_sum / jnp.sum(head_sum, axis=1, keepdims=True)
    for t in range(16):
        wide[4 * t : 4 * t + 4, :] = jnp.broadcast_to(grad[t : t + 1], (4, 2048))
    dk[...] = jnp.zeros_like(dk)

    @pl.loop(0, 4)
    def _(g):
        rows = q_ref[pl.ds(4 * g, 4), 0:64, :].reshape(256, 128)
        z = lax.dot_general(rows, keys[...], NT, preferred_element_type=f32)
        for a in range(4):
            at = a * 64
            value = wide[...] * weight_column(q_ref, 4 * g + a)
            dz[at : at + 64, :] = jnp.where(z[at : at + 64] > 0.0, value, 0.0).astype(bf16)
        dk[...] += lax.dot_general(rows, dz[...], TN, preferred_element_type=f32)
        dq = jnp.dot(dz[...], keys[...], preferred_element_type=f32) * scale
        dq_ref[pl.ds(4 * g, 4)] = dq.astype(bf16).reshape(4, 64, 128)

    for slot in range(16):
        tile = dk[:, slot * 128 : slot * 128 + 128] * scale
        place = lax.div(slot_tile(at_ref, slot), 2)
        if slot % 2 == 0:
            own_ref[place] = tile
        else:
            send_ref[place] = tile.astype(bf16)


def last_body(both_ref, dq_ref, dk_ref):
    for x in range(4):
        total = both_ref[x, 64:96].astype(f32)
        for zh in range(1, 4):
            total += both_ref[4 * zh + x, 64:96].astype(f32)
        dk_ref[:, x * 32 : x * 32 + 32] = total.T
    for j in range(16):
        dq_ref[j] = both_ref[j, 0:64]


def index_backward(at, kept, prob, queries, keys, sums, scale):
    return call(
        functools.partial(back_body, scale),
        (sds((8, 128, 128), f32), sds((8, 128, 128), bf16), sds((16, 64, 128), bf16)),
        [SM, SM] + [VM] * 4,
        16,
        scratch_shapes=[
            pltpu.VMEM((256, 2048), bf16),
            pltpu.VMEM((128, 2048), f32),
            pltpu.VMEM((64, 2048), f32),
        ],
        name="index_backward",
    )(at, kept, prob, queries, keys, sums)


def local(query_latent, key_latent, normalizer, index_query, index_key, index_weight, kept):
    index_scale = index_query.shape[2] ** (-0.5)
    head = lax.axis_index("head")
    seq = lax.axis_index("seq")
    at = jnp.stack([head // 4, head % 4, seq // 4, seq // 2 % 2, seq % 2]).astype(jnp.int32)

    tile = jnp.concatenate([index_key, key_latent.T], axis=0)
    tiles = []
    for u in range(2):
        if u == 1:
            tile = along_z(tile)
        for d in (0,) + STEPS:
            there = along_y(tile, -d) if d else tile
            tiles += [there, other_core(there)]

    w0 = lax.reduce_precision(index_weight, 8, 7)
    w1 = lax.reduce_precision(index_weight - w0, 8, 7)
    w2 = index_weight - w0 - w1
    weight = jnp.stack([w.reshape(16, 64) for w in (w0, w1, w2)], axis=1).astype(bf16)
    weight = jnp.pad(weight, ((0, 0), (0, 13), (0, 64)))
    queries = jnp.concatenate([index_query.reshape(16, 64, 128), weight], axis=1)
    queries = exchanged(queries, "head")

    parts = wide_queries(at, jnp.transpose(query_latent, (1, 2, 0)), normalizer.T)
    query = [parts[0]]
    for part, d in zip(parts[1:], STEPS):
        query.append(along_x(part, d))
    part, index_keys = scores(query[:3], tiles)
    (part,) = scores(query[3:], tiles, part)
    sums = exchanged(part.reshape(4, 16, 2048), "head", ROW_ZH)

    prob = index_forward(at, kept, queries, index_keys, index_scale)
    own, send, dq = index_backward(at, kept, prob, queries, index_keys, sums, index_scale)

    got = other_core(send)
    dkey = (own + got.astype(f32)).astype(bf16)
    dkey = exchanged(dkey.reshape(32, 32, 128), ("seq", "head"), YZX)
    dkey = jnp.sum(dkey.astype(f32), axis=0).astype(bf16)
    dkey = jnp.broadcast_to(dkey, (16, 32, 128))
    both = exchanged(jnp.concatenate([dq, dkey], axis=1), "head")
    dq, dkey = call(
        last_body, (sds((16, 64, 128), bf16), sds((128, 128), f32)), [VM], 6, name="last"
    )(both)
    return dq.reshape(index_query.shape), dkey


def solution(mesh):
    return jax.shard_map(
        local,
        mesh=mesh,
        in_specs=(
            P("seq", "head", None),
            P("seq", None),
            P("seq", "head"),
            P("seq", "head", None),
            P("seq", None),
            P("seq", "head"),
            P("seq", None),
        ),
        out_specs=(P("seq", "head", None), P("seq", None)),
        check_vma=False,
    )
```

```python
import functools

import jax
import jax.numpy as jnp
from jax import lax
from jax.experimental import pallas as pl
from jax.experimental.pallas import tpu as pltpu
from jax.sharding import PartitionSpec as P


attn_scale = 192.0 ** (-0.5)
LOG2E = 1.4426950408889634
STEPS = (1, 3, 2)
f32 = jnp.float32
bf16 = jnp.bfloat16
VM = pl.BlockSpec(memory_space=pltpu.VMEM)
SM = pl.BlockSpec(memory_space=pltpu.SMEM)
HB = pl.BlockSpec(memory_space=pltpu.HBM)

ROW_ZH = [[zh * 4 + x for zh in range(4)] for x in range(4)]
YZX = [
    [(y * 4 + z * 2 + c) * 16 + zh * 4 + x for y in range(4) for z in range(2) for x in range(4)]
    for zh in range(4)
    for c in range(2)
]


def along_y(value, d):
    return lax.ppermute(value, "seq", [(i, (i + 4 * d) % 16) for i in range(16)])


def along_z(value):
    return lax.ppermute(value, "seq", [(i, i ^ 2) for i in range(16)])


def other_core(value):
    return lax.ppermute(value, "seq", [(i, i ^ 1) for i in range(16)])


def along_x(value, d):
    return lax.ppermute(value, "head", [(i, i // 4 * 4 + (i + d) % 4) for i in range(16)])


def exchanged(value, axis, groups=None):
    return lax.all_to_all(value, axis, 0, 0, tiled=True, axis_index_groups=groups)


def sds(shape, dtype):
    return jax.ShapeDtypeStruct(shape, dtype)


def call(body, outs, specs, mib, out_specs=None, **more):
    return pl.pallas_call(
        body,
        out_shape=outs,
        in_specs=specs,
        out_specs=out_specs or jax.tree.map(lambda _: VM, outs),
        compiler_params=pltpu.CompilerParams(vmem_limit_bytes=mib << 20),
        **more,
    )


def query_body(at_ref, q_ref, lse_hbm, o0, o1, o2, o3, wide, turned, lse_ref, in_sem, out_sem):
    heads, width, rows = q_ref.shape
    loads = [
        pltpu.make_async_copy(q_ref.at[h], wide.at[h, 0:width, :], in_sem.at[h]) for h in range(heads)
    ]
    lse_load = pltpu.make_async_copy(lse_hbm, lse_ref, in_sem.at[heads])
    for load in [lse_load] + loads:
        load.start()
    row = lax.broadcasted_iota(jnp.int32, (640 - width, rows), 0)
    lse_load.wait()
    stores = []
    for h in range(heads):
        value = lse_ref[h : h + 1, :] * (-1.0 / attn_scale)
        p0 = value.astype(bf16).astype(f32)
        p1 = (value - p0).astype(bf16).astype(f32)
        p2 = value - p0 - p1
        more = jnp.where(row == 0, p0, jnp.where(row == 1, p1, jnp.where(row == 2, p2, 0.0)))
        wide[h, width:, :] = more.astype(bf16)
        loads[h].wait()
        flat = wide[h].T
        for x in range(4):
            for zh in range(4):
                at = (zh * 4 + x) * 16
                turned[h, x, zh * 16 : zh * 16 + 16, :] = flat[at : at + 16]
        for i, out in enumerate((o0, o1, o2, o3)):
            x = lax.rem(at_ref[1] + ((0,) + STEPS)[i], 4)
            store = pltpu.make_async_copy(turned.at[h, x], out.at[h], out_sem.at[4 * h + i])
            store.start()
            stores.append(store)
    for store in stores:
        store.wait()


def in_hbm(*values):
    return [pltpu.with_memory_space_constraint(v, pltpu.HBM) for v in values]


def wide_queries(at, query, normalizer):
    heads, _, rows = query.shape
    return call(
        query_body,
        (pltpu.HBM((heads, rows // 4, 640), bf16),) * 4,
        [SM, HB, HB],
        12,
        out_specs=(HB,) * 4,
        scratch_shapes=[
            pltpu.VMEM((heads, 640, rows), bf16),
            pltpu.VMEM((heads, 4, rows // 4, 640), bf16),
            pltpu.VMEM((heads, rows), f32),
            pltpu.SemaphoreType.DMA((heads + 1,)),
            pltpu.SemaphoreType.DMA((4 * heads,)),
        ],
        name="wide_queries",
    )(at, *in_hbm(query, normalizer))


def score_body(groups, last, *refs):
    q_hbm, tiles, refs = refs[:groups], refs[groups : groups + 16], refs[groups + 16 :]
    before, (out_ref, *index, q_ref, keys, acc, q_sem) = refs[:last], refs[last:]
    heads, rows, depth = q_ref.shape[1:]
    width = tiles[0].shape[0] - 128
    q_loads = [
        pltpu.make_async_copy(q_hbm[a], q_ref.at[a], q_sem.at[a]) for a in range(groups)
    ]
    for load in q_loads:
        load.start()
    row = lax.broadcasted_iota(jnp.int32, (depth - width, 512), 0)
    for n in range(4):
        keys[n, width:, :] = jnp.where(row < 3, 1.0, 0.0).astype(bf16)
    for index_ref in index:
        for i, tile in enumerate(tiles):
            index_ref[i * 128 : i * 128 + 128, :] = tile[0:128, :]
    for a in range(groups):
        q_loads[a].wait()
        some = q_ref[a].reshape(heads * rows, depth)
        for n in range(4):
            at = n * 512
            for i in range(4) if a == 0 else ():
                keys[n, 0:width, i * 128 : i * 128 + 128] = tiles[4 * n + i][128 : 128 + width, :]
            s = jnp.dot(some, keys[n], preferred_element_type=f32)
            p = jnp.exp2(s * (attn_scale * LOG2E))
            total = acc[:, at : at + 512] if a else None
            for ref in before if a == 0 else ():
                total = ref[:, at : at + 512]
            for h in range(heads):
                part = p[h * rows : h * rows + rows]
                total = part if total is None else total + part
            if a + 1 < groups:
                acc[:, at : at + 512] = total
            else:
                out_ref[:, at : at + 512] = total.astype(out_ref.dtype)


def scores(queries, tiles, *before):
    heads, rows, depth = queries[0].shape
    groups, last = len(queries), len(before)
    return call(
        functools.partial(score_body, groups, last),
        (sds((rows, 2048), bf16),) if last else (sds((rows, 2048), f32), sds((2048, 128), bf16)),
        [HB] * groups + [VM] * (16 + last),
        16,
        scratch_shapes=[
            pltpu.VMEM((groups, heads, rows, depth), bf16),
            pltpu.VMEM((4, depth, 512), bf16),
            pltpu.VMEM((rows, 2048), f32),
            pltpu.SemaphoreType.DMA((groups,)),
        ],
        name="scores",
    )(*in_hbm(*queries), *tiles, *before)


def pack_body(q_ref, w_ref, out_ref):
    value = w_ref[...]
    p0 = value.astype(bf16).astype(f32)
    p1 = (value - p0).astype(bf16).astype(f32)
    p2 = value - p0 - p1
    rows = jnp.concatenate([p0, p1, p2, jnp.zeros_like(p0)], axis=0).astype(bf16)
    for j in range(16):
        out_ref[j, 0:64, :] = q_ref[j]
        out_ref[j, 64:80, :] = rows[:, j // 8 * 128 : j // 8 * 128 + 128]


def weight_column(at_ref, q_ref, j):
    block = lax.rem(at_ref[0] * 4 + at_ref[1], 8) * 16
    rows = q_ref[j, 64:80, :].astype(f32)
    rows = rows[0:4] + rows[4:8] + rows[8:12]
    rows = jnp.concatenate([rows] * 16, axis=0)
    lane = lax.broadcasted_iota(jnp.int32, (64, 128), 1)
    query = lax.broadcasted_iota(jnp.int32, (64, 128), 0) // 4
    return jnp.sum(jnp.where(lane == query + block, rows, 0.0), axis=1, keepdims=True)


def slot_tile(at_ref, slot):
    u, k, v = slot // 8, slot // 2 % 4, slot % 2
    y = lax.rem(at_ref[2] + ((0,) + STEPS)[k], 4)
    z = at_ref[3] if u == 0 else 1 - at_ref[3]
    c = at_ref[4] if v == 0 else 1 - at_ref[4]
    return y * 4 + z * 2 + c


def allowed(at_ref, kept_ref):
    half = jnp.where(at_ref[0] >= 2, 1, 0)
    flags = [
        jnp.full((16, 128), kept_ref[half, slot_tile(at_ref, slot)], jnp.int32) for slot in range(16)
    ]
    return jnp.concatenate(flags, axis=1) > 0


NT = (((1,), (1,)), ((), ()))
TN = (((0,), (0,)), ((), ()))


def index_body(scale, at_ref, kept_ref, q_ref, keys, prob_ref, acc):
    acc[...] = jnp.zeros_like(acc)

    @pl.loop(0, 4)
    def _(g):
        rows = q_ref[pl.ds(4 * g, 4), 0:64, :].reshape(256, 128)
        z = lax.dot_general(rows, keys[...], NT, preferred_element_type=f32)
        part = None
        for a in range(4):
            weight = weight_column(at_ref, q_ref, 4 * g + a) * scale
            term = jnp.maximum(z[a * 64 : a * 64 + 64], 0.0) * weight
            part = term if part is None else part + term
        acc[...] += part

    pick = (
        lax.broadcasted_iota(jnp.int32, (16, 64), 1) // 4
        == lax.broadcasted_iota(jnp.int32, (16, 64), 0)
    ).astype(f32)
    logit = jnp.dot(pick, acc[...], precision=lax.Precision.HIGHEST, preferred_element_type=f32)
    keep = allowed(at_ref, kept_ref)
    top = jnp.max(jnp.where(keep, logit, -jnp.inf), axis=1, keepdims=True)
    expo = jnp.where(keep, jnp.exp(jnp.where(keep, logit, top) - top), 0.0)
    prob_ref[...] = expo / jnp.sum(expo, axis=1, keepdims=True)


def index_forward(at, kept, queries, keys, scale):
    return call(
        functools.partial(index_body, scale),
        sds((16, 2048), f32),
        [SM, SM, VM, VM],
        14,
        scratch_shapes=[pltpu.VMEM((64, 2048), f32)],
        name="index_forward",
    )(at, kept, queries, keys)


def back_body(scale, at_ref, kept_ref, prob_ref, q_ref, keys, sums, *refs):
    own_ref, send_ref, dq_ref, dz, dk, wide = refs
    total = sums[0].astype(f32)
    for j in range(1, sums.shape[0]):
        total += sums[j].astype(f32)
    head_sum = jnp.where(allowed(at_ref, kept_ref), total, 0.0)
    grad = prob_ref[...] - head_sum / jnp.sum(head_sum, axis=1, keepdims=True)
    for t in range(16):
        wide[4 * t : 4 * t + 4, :] = jnp.broadcast_to(grad[t : t + 1], (4, 2048))
    for g in range(4):
        rows = q_ref[4 * g : 4 * g + 4, 0:64, :].reshape(256, 128)
        z = lax.dot_general(rows, keys[...], NT, preferred_element_type=f32)
        for a in range(4):
            at = a * 64
            value = wide[...] * weight_column(at_ref, q_ref, 4 * g + a)
            dz[g % 2, at : at + 64, :] = jnp.where(z[at : at + 64] > 0.0, value, 0.0).astype(bf16)
        part = lax.dot_general(rows, dz[g % 2], TN, preferred_element_type=f32)
        dk[...] = part if g == 0 else dk[...] + part
        dq = jnp.dot(dz[g % 2], keys[...], preferred_element_type=f32) * scale
        dq_ref[4 * g : 4 * g + 4] = dq.astype(bf16).reshape(4, 64, 128)

    for slot in range(16):
        tile = dk[:, slot * 128 : slot * 128 + 128] * scale
        place = lax.div(slot_tile(at_ref, slot), 2)
        if slot % 2 == 0:
            own_ref[place] = tile
        else:
            send_ref[place] = tile.astype(bf16)


def last_body(both_ref, dq_ref, dk_ref):
    for x in range(4):
        total = both_ref[x, 64:96].astype(f32)
        for zh in range(1, 4):
            total += both_ref[4 * zh + x, 64:96].astype(f32)
        dk_ref[:, x * 32 : x * 32 + 32] = total.T
    for j in range(16):
        dq_ref[j] = both_ref[j, 0:64]


def index_backward(at, kept, prob, queries, keys, sums, scale):
    return call(
        functools.partial(back_body, scale),
        (sds((8, 128, 128), f32), sds((8, 128, 128), bf16), sds((16, 64, 128), bf16)),
        [SM, SM] + [VM] * 4,
        16,
        scratch_shapes=[
            pltpu.VMEM((2, 256, 2048), bf16),
            pltpu.VMEM((128, 2048), f32),
            pltpu.VMEM((64, 2048), f32),
        ],
        name="index_backward",
    )(at, kept, prob, queries, keys, sums)


def local(query_latent, key_latent, normalizer, index_query, index_key, index_weight, kept):
    index_scale = index_query.shape[2] ** (-0.5)
    head = lax.axis_index("head")
    seq = lax.axis_index("seq")
    at = jnp.stack([head // 4, head % 4, seq // 4, seq // 2 % 2, seq % 2]).astype(jnp.int32)

    tile = jnp.concatenate([index_key, key_latent.T], axis=0)
    tiles = []
    for u in range(2):
        if u == 1:
            tile = along_z(tile)
        for d in (0,) + STEPS:
            there = along_y(tile, -d) if d else tile
            tiles += [there, other_core(there)]

    queries = call(
        pack_body, pltpu.HBM((16, 80, 128), bf16), [VM, VM], 6, out_specs=VM, name="pack"
    )(index_query.reshape(16, 64, 128), index_weight.T)
    queries = exchanged(queries, "head")

    parts = wide_queries(at, jnp.transpose(query_latent, (1, 2, 0)), normalizer.T)
    query = [parts[0]]
    for part, d in zip(parts[1:], STEPS):
        query.append(along_x(part, d))
    part, index_keys = scores(query[:3], tiles)
    (part,) = scores(query[3:], tiles, part)
    sums = exchanged(part.reshape(4, 16, 2048), "head", ROW_ZH)

    prob = index_forward(at, kept, queries, index_keys, index_scale)
    own, send, dq = index_backward(at, kept, prob, queries, index_keys, sums, index_scale)

    got = other_core(send)
    dkey = (own + got.astype(f32)).astype(bf16)
    dkey = exchanged(dkey.reshape(32, 32, 128), ("seq", "head"), YZX)
    dkey = jnp.sum(dkey.astype(f32), axis=0).astype(bf16)
    dkey = jnp.broadcast_to(dkey, (16, 32, 128))
    both = exchanged(jnp.concatenate([dq, dkey], axis=1), "head")
    dq, dkey = call(
        last_body, (sds((16, 64, 128), bf16), sds((128, 128), f32)), [VM], 6, name="last"
    )(both)
    return dq.reshape(index_query.shape), dkey


def solution(mesh):
    return jax.shard_map(
        local,
        mesh=mesh,
        in_specs=(
            P("seq", "head", None),
            P("seq", None),
            P("seq", "head"),
            P("seq", "head", None),
            P("seq", None),
            P("seq", "head"),
            P("seq", None),
        ),
        out_specs=(P("seq", "head", None), P("seq", None)),
        check_vma=False,
    )
```

```python
import functools

import jax
import jax.numpy as jnp
from jax import lax
from jax.experimental import pallas as pl
from jax.experimental.pallas import tpu as pltpu
from jax.sharding import PartitionSpec as P


attn_scale = 192.0 ** (-0.5)
LOG2E = 1.4426950408889634
STEPS = (1, 3, 2)
f32 = jnp.float32
bf16 = jnp.bfloat16
VM = pl.BlockSpec(memory_space=pltpu.VMEM)
SM = pl.BlockSpec(memory_space=pltpu.SMEM)
HB = pl.BlockSpec(memory_space=pltpu.HBM)

ROW_ZH = [[zh * 4 + x for zh in range(4)] for x in range(4)]
SAME_ZH = [[seq * 16 + zh * 4 + x for seq in range(16) for x in range(4)] for zh in range(4)]


def along_y(value, d):
    return lax.ppermute(value, "seq", [(i, (i + 4 * d) % 16) for i in range(16)])


def along_z(value):
    return lax.ppermute(value, "seq", [(i, i ^ 2) for i in range(16)])


def other_core(value):
    return lax.ppermute(value, "seq", [(i, i ^ 1) for i in range(16)])


def along_x(value, d):
    return lax.ppermute(value, "head", [(i, i // 4 * 4 + (i + d) % 4) for i in range(16)])


def exchanged(value, axis, groups=None):
    return lax.all_to_all(value, axis, 0, 0, tiled=True, axis_index_groups=groups)


def sds(shape, dtype):
    return jax.ShapeDtypeStruct(shape, dtype)


def call(body, outs, specs, mib, out_specs=None, **more):
    return pl.pallas_call(
        body,
        out_shape=outs,
        in_specs=specs,
        out_specs=out_specs or jax.tree.map(lambda _: VM, outs),
        compiler_params=pltpu.CompilerParams(vmem_limit_bytes=mib << 20),
        **more,
    )


def query_body(at_ref, q_ref, lse_hbm, o0, o1, o2, o3, wide, turned, lse_ref, in_sem, out_sem):
    heads, width, rows = q_ref.shape
    loads = [
        pltpu.make_async_copy(q_ref.at[h], wide.at[h, 0:width, :], in_sem.at[h]) for h in range(heads)
    ]
    lse_load = pltpu.make_async_copy(lse_hbm, lse_ref, in_sem.at[heads])
    for load in [lse_load] + loads:
        load.start()
    row = lax.broadcasted_iota(jnp.int32, (640 - width, rows), 0)
    lse_load.wait()
    stores = []
    for h in range(heads):
        value = lse_ref[h : h + 1, :] * (-1.0 / attn_scale)
        p0 = value.astype(bf16).astype(f32)
        p1 = (value - p0).astype(bf16).astype(f32)
        p2 = value - p0 - p1
        more = jnp.where(row == 0, p0, jnp.where(row == 1, p1, jnp.where(row == 2, p2, 0.0)))
        wide[h, width:, :] = more.astype(bf16)
        loads[h].wait()
        flat = wide[h].T
        for x in range(4):
            for zh in range(4):
                at = (zh * 4 + x) * 16
                turned[h, x, zh * 16 : zh * 16 + 16, :] = flat[at : at + 16]
        for i, out in enumerate((o0, o1, o2, o3)):
            x = lax.rem(at_ref[1] + ((0,) + STEPS)[i], 4)
            store = pltpu.make_async_copy(turned.at[h, x], out.at[h], out_sem.at[4 * h + i])
            store.start()
            stores.append(store)
    for store in stores:
        store.wait()


def in_hbm(*values):
    return [pltpu.with_memory_space_constraint(v, pltpu.HBM) for v in values]


def wide_queries(at, query, normalizer):
    heads, _, rows = query.shape
    return call(
        query_body,
        (pltpu.HBM((heads, rows // 4, 640), bf16),) * 4,
        [SM, HB, HB],
        12,
        out_specs=(HB,) * 4,
        scratch_shapes=[
            pltpu.VMEM((heads, 640, rows), bf16),
            pltpu.VMEM((heads, 4, rows // 4, 640), bf16),
            pltpu.VMEM((heads, rows), f32),
            pltpu.SemaphoreType.DMA((heads + 1,)),
            pltpu.SemaphoreType.DMA((4 * heads,)),
        ],
        name="wide_queries",
    )(at, *in_hbm(query, normalizer))


def score_body(groups, last, *refs):
    q_hbm, tiles, refs = refs[:groups], refs[groups : groups + 16], refs[groups + 16 :]
    before, (out_ref, *index, q_ref, keys, acc, q_sem) = refs[:last], refs[last:]
    heads, rows, depth = q_ref.shape[1:]
    width = tiles[0].shape[0] - 128
    q_loads = [
        pltpu.make_async_copy(q_hbm[a], q_ref.at[a], q_sem.at[a]) for a in range(groups)
    ]
    for load in q_loads:
        load.start()
    row = lax.broadcasted_iota(jnp.int32, (depth - width, 512), 0)
    for n in range(4):
        keys[n, width:, :] = jnp.where(row < 3, 1.0, 0.0).astype(bf16)
    for index_ref in index:
        for i, tile in enumerate(tiles):
            index_ref[i * 128 : i * 128 + 128, :] = tile[0:128, :]
    for a in range(groups):
        q_loads[a].wait()
        some = q_ref[a].reshape(heads * rows, depth)
        for n in range(4):
            at = n * 512
            for i in range(4) if a == 0 else ():
                keys[n, 0:width, i * 128 : i * 128 + 128] = tiles[4 * n + i][128 : 128 + width, :]
            s = jnp.dot(some, keys[n], preferred_element_type=f32)
            p = jnp.exp2(s * (attn_scale * LOG2E))
            total = acc[:, at : at + 512] if a else None
            for ref in before if a == 0 else ():
                total = ref[:, at : at + 512]
            for h in range(heads):
                part = p[h * rows : h * rows + rows]
                total = part if total is None else total + part
            if a + 1 < groups:
                acc[:, at : at + 512] = total
            else:
                out_ref[:, at : at + 512] = total.astype(out_ref.dtype)


def scores(queries, tiles, *before):
    heads, rows, depth = queries[0].shape
    groups, last = len(queries), len(before)
    return call(
        functools.partial(score_body, groups, last),
        (sds((rows, 2048), bf16),) if last else (sds((rows, 2048), f32), sds((2048, 128), bf16)),
        [HB] * groups + [VM] * (16 + last),
        16,
        scratch_shapes=[
            pltpu.VMEM((groups, heads, rows, depth), bf16),
            pltpu.VMEM((4, depth, 512), bf16),
            pltpu.VMEM((rows, 2048), f32),
            pltpu.SemaphoreType.DMA((groups,)),
        ],
        name="scores",
    )(*in_hbm(*queries), *tiles, *before)


def pack_body(q_ref, w_ref, out_ref):
    value = w_ref[...]
    p0 = value.astype(bf16).astype(f32)
    p1 = (value - p0).astype(bf16).astype(f32)
    p2 = value - p0 - p1
    rows = jnp.concatenate([p0, p1, p2, jnp.zeros_like(p0)], axis=0).astype(bf16)
    for j in range(16):
        out_ref[j, 0:64, :] = q_ref[j]
        out_ref[j, 64:80, :] = rows[:, j // 8 * 128 : j // 8 * 128 + 128]


def weight_column(at_ref, q_ref, j):
    block = lax.rem(at_ref[0] * 4 + at_ref[1], 8) * 16
    rows = q_ref[j, 64:80, :].astype(f32)
    rows = rows[0:4] + rows[4:8] + rows[8:12]
    rows = jnp.concatenate([rows] * 16, axis=0)
    lane = lax.broadcasted_iota(jnp.int32, (64, 128), 1)
    query = lax.broadcasted_iota(jnp.int32, (64, 128), 0) // 4
    return jnp.sum(jnp.where(lane == query + block, rows, 0.0), axis=1, keepdims=True)


def slot_tile(at_ref, slot):
    u, k, v = slot // 8, slot // 2 % 4, slot % 2
    y = lax.rem(at_ref[2] + ((0,) + STEPS)[k], 4)
    z = at_ref[3] if u == 0 else 1 - at_ref[3]
    c = at_ref[4] if v == 0 else 1 - at_ref[4]
    return y * 4 + z * 2 + c


def allowed(at_ref, kept_ref):
    half = jnp.where(at_ref[0] >= 2, 1, 0)
    flags = [
        jnp.full((16, 128), kept_ref[half, slot_tile(at_ref, slot)], jnp.int32) for slot in range(16)
    ]
    return jnp.concatenate(flags, axis=1) > 0


NT = (((1,), (1,)), ((), ()))
TN = (((0,), (0,)), ((), ()))


def index_body(scale, at_ref, kept_ref, q_ref, keys, prob_ref, acc):
    acc[...] = jnp.zeros_like(acc)

    @pl.loop(0, 4)
    def _(g):
        rows = q_ref[pl.ds(4 * g, 4), 0:64, :].reshape(256, 128)
        z = lax.dot_general(rows, keys[...], NT, preferred_element_type=f32)
        part = None
        for a in range(4):
            weight = weight_column(at_ref, q_ref, 4 * g + a) * scale
            term = jnp.maximum(z[a * 64 : a * 64 + 64], 0.0) * weight
            part = term if part is None else part + term
        acc[...] += part

    pick = (
        lax.broadcasted_iota(jnp.int32, (16, 64), 1) // 4
        == lax.broadcasted_iota(jnp.int32, (16, 64), 0)
    ).astype(f32)
    logit = jnp.dot(pick, acc[...], precision=lax.Precision.HIGHEST, preferred_element_type=f32)
    keep = allowed(at_ref, kept_ref)
    top = jnp.max(jnp.where(keep, logit, -jnp.inf), axis=1, keepdims=True)
    expo = jnp.where(keep, jnp.exp(jnp.where(keep, logit, top) - top), 0.0)
    prob_ref[...] = expo / jnp.sum(expo, axis=1, keepdims=True)


def index_forward(at, kept, queries, keys, scale):
    return call(
        functools.partial(index_body, scale),
        sds((16, 2048), f32),
        [SM, SM, VM, VM],
        14,
        scratch_shapes=[pltpu.VMEM((64, 2048), f32)],
        name="index_forward",
    )(at, kept, queries, keys)


def back_body(scale, at_ref, kept_ref, prob_ref, q_ref, keys, sums, *refs):
    dk_ref, dq_ref, dz, dk, wide = refs
    total = sums[0].astype(f32)
    for j in range(1, sums.shape[0]):
        total += sums[j].astype(f32)
    head_sum = jnp.where(allowed(at_ref, kept_ref), total, 0.0)
    grad = prob_ref[...] - head_sum / jnp.sum(head_sum, axis=1, keepdims=True)
    for t in range(16):
        wide[4 * t : 4 * t + 4, :] = jnp.broadcast_to(grad[t : t + 1], (4, 2048))
    for g in range(4):
        rows = q_ref[4 * g : 4 * g + 4, 0:64, :].reshape(256, 128)
        z = lax.dot_general(rows, keys[...], NT, preferred_element_type=f32)
        for a in range(4):
            at = a * 64
            value = wide[...] * weight_column(at_ref, q_ref, 4 * g + a)
            dz[g % 2, at : at + 64, :] = jnp.where(z[at : at + 64] > 0.0, value, 0.0).astype(bf16)
        part = lax.dot_general(rows, dz[g % 2], TN, preferred_element_type=f32)
        dk[...] = part if g == 0 else dk[...] + part
        dq = jnp.dot(dz[g % 2], keys[...], preferred_element_type=f32) * scale
        dq_ref[4 * g : 4 * g + 4] = dq.astype(bf16).reshape(4, 64, 128)

    for slot in range(16):
        tile = dk[:, slot * 128 : slot * 128 + 128] * scale
        dk_ref[slot_tile(at_ref, slot)] = tile.astype(bf16)


def last_body(both_ref, dq_ref, dk_ref):
    for x in range(4):
        total = both_ref[x, 64:96].astype(f32)
        for zh in range(1, 4):
            total += both_ref[4 * zh + x, 64:96].astype(f32)
        dk_ref[:, x * 32 : x * 32 + 32] = total.T
    for j in range(16):
        dq_ref[j] = both_ref[j, 0:64]


def index_backward(at, kept, prob, queries, keys, sums, scale):
    return call(
        functools.partial(back_body, scale),
        (sds((16, 128, 128), bf16), sds((16, 64, 128), bf16)),
        [SM, SM] + [VM] * 4,
        16,
        scratch_shapes=[
            pltpu.VMEM((2, 256, 2048), bf16),
            pltpu.VMEM((128, 2048), f32),
            pltpu.VMEM((64, 2048), f32),
        ],
        name="index_backward",
    )(at, kept, prob, queries, keys, sums)


def local(query_latent, key_latent, normalizer, index_query, index_key, index_weight, kept):
    index_scale = index_query.shape[2] ** (-0.5)
    head = lax.axis_index("head")
    seq = lax.axis_index("seq")
    at = jnp.stack([head // 4, head % 4, seq // 4, seq // 2 % 2, seq % 2]).astype(jnp.int32)

    tile = jnp.concatenate([index_key, key_latent.T], axis=0)
    tiles = []
    for u in range(2):
        if u == 1:
            tile = along_z(tile)
        for d in (0,) + STEPS:
            there = along_y(tile, -d) if d else tile
            tiles += [there, other_core(there)]

    queries = call(
        pack_body, pltpu.HBM((16, 80, 128), bf16), [VM, VM], 6, out_specs=VM, name="pack"
    )(index_query.reshape(16, 64, 128), index_weight.T)
    queries = exchanged(queries, "head")

    parts = wide_queries(at, jnp.transpose(query_latent, (1, 2, 0)), normalizer.T)
    query = [parts[0]]
    for part, d in zip(parts[1:], STEPS):
        query.append(along_x(part, d))
    part, index_keys = scores(query[:1], tiles)
    (part,) = scores(query[1:], tiles, part)
    sums = exchanged(part.reshape(4, 16, 2048), "head", ROW_ZH)

    prob = index_forward(at, kept, queries, index_keys, index_scale)
    dkey, dq = index_backward(at, kept, prob, queries, index_keys, sums, index_scale)

    dkey = exchanged(dkey.reshape(64, 32, 128), ("seq", "head"), SAME_ZH)
    dkey = jnp.sum(dkey.astype(f32), axis=0).astype(bf16)
    dkey = jnp.broadcast_to(dkey, (16, 32, 128))
    both = exchanged(jnp.concatenate([dq, dkey], axis=1), "head")
    dq, dkey = call(
        last_body, (sds((16, 64, 128), bf16), sds((128, 128), f32)), [VM], 6, name="last"
    )(both)
    return dq.reshape(index_query.shape), dkey


def solution(mesh):
    return jax.shard_map(
        local,
        mesh=mesh,
        in_specs=(
            P("seq", "head", None),
            P("seq", None),
            P("seq", "head"),
            P("seq", "head", None),
            P("seq", None),
            P("seq", "head"),
            P("seq", None),
        ),
        out_specs=(P("seq", "head", None), P("seq", None)),
        check_vma=False,
    )
```

```python
import functools

import jax
import jax.numpy as jnp
from jax import lax
from jax.experimental import pallas as pl
from jax.experimental.pallas import tpu as pltpu
from jax.sharding import PartitionSpec as P


attn_scale = 192.0 ** (-0.5)
LOG2E = 1.4426950408889634
STEPS = (1, 3, 2)
f32 = jnp.float32
bf16 = jnp.bfloat16
VM = pl.BlockSpec(memory_space=pltpu.VMEM)
SM = pl.BlockSpec(memory_space=pltpu.SMEM)
HB = pl.BlockSpec(memory_space=pltpu.HBM)

ROW_ZH = [[zh * 4 + x for zh in range(4)] for x in range(4)]
YZX = [
    [(y * 4 + z * 2 + c) * 16 + zh * 4 + x for y in range(4) for z in range(2) for x in range(4)]
    for zh in range(4)
    for c in range(2)
]


def along_y(value, d):
    return lax.ppermute(value, "seq", [(i, (i + 4 * d) % 16) for i in range(16)])


def along_z(value):
    return lax.ppermute(value, "seq", [(i, i ^ 2) for i in range(16)])


def other_core(value):
    return lax.ppermute(value, "seq", [(i, i ^ 1) for i in range(16)])


def along_x(value, d):
    return lax.ppermute(value, "head", [(i, i // 4 * 4 + (i + d) % 4) for i in range(16)])


def exchanged(value, axis, groups=None):
    return lax.all_to_all(value, axis, 0, 0, tiled=True, axis_index_groups=groups)


def sds(shape, dtype):
    return jax.ShapeDtypeStruct(shape, dtype)


def call(body, outs, specs, mib, out_specs=None, **more):
    return pl.pallas_call(
        body,
        out_shape=outs,
        in_specs=specs,
        out_specs=out_specs or jax.tree.map(lambda _: VM, outs),
        compiler_params=pltpu.CompilerParams(vmem_limit_bytes=mib << 20),
        **more,
    )


def query_body(at_ref, q_ref, lse_hbm, o0, o1, o2, o3, wide, turned, lse_ref, in_sem, out_sem):
    heads, width, rows = q_ref.shape
    loads = [
        pltpu.make_async_copy(q_ref.at[h], wide.at[h, 0:width, :], in_sem.at[h]) for h in range(heads)
    ]
    lse_load = pltpu.make_async_copy(lse_hbm, lse_ref, in_sem.at[heads])
    for load in [lse_load] + loads:
        load.start()
    row = lax.broadcasted_iota(jnp.int32, (640 - width, rows), 0)
    lse_load.wait()
    stores = []
    for h in range(heads):
        value = lse_ref[h : h + 1, :] * (-1.0 / attn_scale)
        p0 = value.astype(bf16).astype(f32)
        p1 = (value - p0).astype(bf16).astype(f32)
        p2 = value - p0 - p1
        more = jnp.where(row == 0, p0, jnp.where(row == 1, p1, jnp.where(row == 2, p2, 0.0)))
        wide[h, width:, :] = more.astype(bf16)
        loads[h].wait()
        flat = wide[h].T
        for x in range(4):
            for zh in range(4):
                at = (zh * 4 + x) * 16
                turned[h, x, zh * 16 : zh * 16 + 16, :] = flat[at : at + 16]
        for i, out in enumerate((o0, o1, o2, o3)):
            x = lax.rem(at_ref[1] + ((0,) + STEPS)[i], 4)
            store = pltpu.make_async_copy(turned.at[h, x], out.at[h], out_sem.at[4 * h + i])
            store.start()
            stores.append(store)
    for store in stores:
        store.wait()


def in_hbm(*values):
    return [pltpu.with_memory_space_constraint(v, pltpu.HBM) for v in values]


def wide_queries(at, query, normalizer):
    heads, _, rows = query.shape
    return call(
        query_body,
        (pltpu.HBM((heads, rows // 4, 640), bf16),) * 4,
        [SM, HB, HB],
        12,
        out_specs=(HB,) * 4,
        scratch_shapes=[
            pltpu.VMEM((heads, 640, rows), bf16),
            pltpu.VMEM((heads, 4, rows // 4, 640), bf16),
            pltpu.VMEM((heads, rows), f32),
            pltpu.SemaphoreType.DMA((heads + 1,)),
            pltpu.SemaphoreType.DMA((4 * heads,)),
        ],
        name="wide_queries",
    )(at, *in_hbm(query, normalizer))


def score_body(groups, last, *refs):
    q_hbm, tiles, refs = refs[:groups], refs[groups : groups + 16], refs[groups + 16 :]
    before, (out_ref, *index, q_ref, keys, acc, q_sem) = refs[:last], refs[last:]
    heads, rows, depth = q_ref.shape[1:]
    width = tiles[0].shape[0] - 128
    q_loads = [
        pltpu.make_async_copy(q_hbm[a], q_ref.at[a], q_sem.at[a]) for a in range(groups)
    ]
    for load in q_loads:
        load.start()
    row = lax.broadcasted_iota(jnp.int32, (depth - width, 512), 0)
    for n in range(4):
        keys[n, width:, :] = jnp.where(row < 3, 1.0, 0.0).astype(bf16)
    for index_ref in index:
        for i, tile in enumerate(tiles):
            index_ref[i * 128 : i * 128 + 128, :] = tile[0:128, :]
    for a in range(groups):
        q_loads[a].wait()
        some = q_ref[a].reshape(heads * rows, depth)
        for n in range(4):
            at = n * 512
            for i in range(4) if a == 0 else ():
                keys[n, 0:width, i * 128 : i * 128 + 128] = tiles[4 * n + i][128 : 128 + width, :]
            s = jnp.dot(some, keys[n], preferred_element_type=f32)
            p = jnp.exp2(s * (attn_scale * LOG2E))
            total = acc[:, at : at + 512] if a else None
            for ref in before if a == 0 else ():
                total = ref[:, at : at + 512]
            for h in range(heads):
                part = p[h * rows : h * rows + rows]
                total = part if total is None else total + part
            if a + 1 < groups:
                acc[:, at : at + 512] = total
            else:
                out_ref[:, at : at + 512] = total.astype(out_ref.dtype)


def scores(queries, tiles, *before):
    heads, rows, depth = queries[0].shape
    groups, last = len(queries), len(before)
    return call(
        functools.partial(score_body, groups, last),
        (sds((rows, 2048), bf16),) if last else (sds((rows, 2048), f32), sds((2048, 128), bf16)),
        [pl.BlockSpec(memory_space=pl.ANY) if last else HB] * groups + [VM] * (16 + last),
        16,
        scratch_shapes=[
            pltpu.VMEM((groups, heads, rows, depth), bf16),
            pltpu.VMEM((4, depth, 512), bf16),
            pltpu.VMEM((rows, 2048), f32),
            pltpu.SemaphoreType.DMA((groups,)),
        ],
        name="scores",
    )(*(queries if last else in_hbm(*queries)), *tiles, *before)


def pack_body(q_ref, w_ref, out_ref):
    value = w_ref[...]
    p0 = value.astype(bf16).astype(f32)
    p1 = (value - p0).astype(bf16).astype(f32)
    p2 = value - p0 - p1
    rows = jnp.concatenate([p0, p1, p2, jnp.zeros_like(p0)], axis=0).astype(bf16)
    for j in range(16):
        out_ref[j, 0:64, :] = q_ref[j]
        out_ref[j, 64:80, :] = rows[:, j // 8 * 128 : j // 8 * 128 + 128]


def weight_column(at_ref, q_ref, j):
    block = lax.rem(at_ref[0] * 4 + at_ref[1], 8) * 16
    rows = q_ref[j, 64:80, :].astype(f32)
    rows = rows[0:4] + rows[4:8] + rows[8:12]
    rows = jnp.concatenate([rows] * 16, axis=0)
    lane = lax.broadcasted_iota(jnp.int32, (64, 128), 1)
    query = lax.broadcasted_iota(jnp.int32, (64, 128), 0) // 4
    return jnp.sum(jnp.where(lane == query + block, rows, 0.0), axis=1, keepdims=True)


def slot_tile(at_ref, slot):
    u, k, v = slot // 8, slot // 2 % 4, slot % 2
    y = lax.rem(at_ref[2] + ((0,) + STEPS)[k], 4)
    z = at_ref[3] if u == 0 else 1 - at_ref[3]
    c = at_ref[4] if v == 0 else 1 - at_ref[4]
    return y * 4 + z * 2 + c


def allowed(at_ref, kept_ref):
    half = jnp.where(at_ref[0] >= 2, 1, 0)
    flags = [
        jnp.full((16, 128), kept_ref[half, slot_tile(at_ref, slot)], jnp.int32) for slot in range(16)
    ]
    return jnp.concatenate(flags, axis=1) > 0


NT = (((1,), (1,)), ((), ()))
TN = (((0,), (0,)), ((), ()))


def index_body(scale, at_ref, kept_ref, q_ref, keys, prob_ref, acc):
    acc[...] = jnp.zeros_like(acc)

    @pl.loop(0, 4)
    def _(g):
        rows = q_ref[pl.ds(4 * g, 4), 0:64, :].reshape(256, 128)
        z = lax.dot_general(rows, keys[...], NT, preferred_element_type=f32)
        part = None
        for a in range(4):
            weight = weight_column(at_ref, q_ref, 4 * g + a) * scale
            term = jnp.maximum(z[a * 64 : a * 64 + 64], 0.0) * weight
            part = term if part is None else part + term
        acc[...] += part

    pick = (
        lax.broadcasted_iota(jnp.int32, (16, 64), 1) // 4
        == lax.broadcasted_iota(jnp.int32, (16, 64), 0)
    ).astype(f32)
    logit = jnp.dot(pick, acc[...], precision=lax.Precision.HIGHEST, preferred_element_type=f32)
    keep = allowed(at_ref, kept_ref)
    top = jnp.max(jnp.where(keep, logit, -jnp.inf), axis=1, keepdims=True)
    expo = jnp.where(keep, jnp.exp(jnp.where(keep, logit, top) - top), 0.0)
    prob_ref[...] = expo / jnp.sum(expo, axis=1, keepdims=True)


def index_forward(at, kept, queries, keys, scale):
    return call(
        functools.partial(index_body, scale),
        sds((16, 2048), f32),
        [SM, SM, VM, VM],
        14,
        scratch_shapes=[pltpu.VMEM((64, 2048), f32)],
        name="index_forward",
    )(at, kept, queries, keys)


def back_body(scale, at_ref, kept_ref, prob_ref, q_ref, keys, sums, *refs):
    own_ref, send_ref, dq_ref, dz, dk, wide = refs
    total = sums[0].astype(f32)
    for j in range(1, sums.shape[0]):
        total += sums[j].astype(f32)
    head_sum = jnp.where(allowed(at_ref, kept_ref), total, 0.0)
    grad = prob_ref[...] - head_sum / jnp.sum(head_sum, axis=1, keepdims=True)
    for t in range(16):
        wide[4 * t : 4 * t + 4, :] = jnp.broadcast_to(grad[t : t + 1], (4, 2048))
    for g in range(4):
        rows = q_ref[4 * g : 4 * g + 4, 0:64, :].reshape(256, 128)
        z = lax.dot_general(rows, keys[...], NT, preferred_element_type=f32)
        for a in range(4):
            at = a * 64
            value = wide[...] * weight_column(at_ref, q_ref, 4 * g + a)
            dz[g % 2, at : at + 64, :] = jnp.where(z[at : at + 64] > 0.0, value, 0.0).astype(bf16)
        part = lax.dot_general(rows, dz[g % 2], TN, preferred_element_type=f32)
        dk[...] = part if g == 0 else dk[...] + part
        dq = jnp.dot(dz[g % 2], keys[...], preferred_element_type=f32) * scale
        dq_ref[4 * g : 4 * g + 4] = dq.astype(bf16).reshape(4, 64, 128)

    for slot in range(16):
        tile = dk[:, slot * 128 : slot * 128 + 128] * scale
        place = lax.div(slot_tile(at_ref, slot), 2)
        if slot % 2 == 0:
            own_ref[place] = tile
        else:
            send_ref[place] = tile.astype(bf16)


def last_body(both_ref, dq_ref, dk_ref):
    for x in range(4):
        total = both_ref[x, 64:96].astype(f32)
        for zh in range(1, 4):
            total += both_ref[4 * zh + x, 64:96].astype(f32)
        dk_ref[:, x * 32 : x * 32 + 32] = total.T
    for j in range(16):
        dq_ref[j] = both_ref[j, 0:64]


def index_backward(at, kept, prob, queries, keys, sums, scale):
    return call(
        functools.partial(back_body, scale),
        (sds((8, 128, 128), f32), sds((8, 128, 128), bf16), sds((16, 64, 128), bf16)),
        [SM, SM] + [VM] * 4,
        16,
        scratch_shapes=[
            pltpu.VMEM((2, 256, 2048), bf16),
            pltpu.VMEM((128, 2048), f32),
            pltpu.VMEM((64, 2048), f32),
        ],
        name="index_backward",
    )(at, kept, prob, queries, keys, sums)


def local(query_latent, key_latent, normalizer, index_query, index_key, index_weight, kept):
    index_scale = index_query.shape[2] ** (-0.5)
    head = lax.axis_index("head")
    seq = lax.axis_index("seq")
    at = jnp.stack([head // 4, head % 4, seq // 4, seq // 2 % 2, seq % 2]).astype(jnp.int32)

    tile = jnp.concatenate([index_key, key_latent.T], axis=0)
    tiles = []
    for u in range(2):
        if u == 1:
            tile = along_z(tile)
        for d in (0,) + STEPS:
            there = along_y(tile, -d) if d else tile
            tiles += [there, other_core(there)]

    queries = call(
        pack_body, pltpu.HBM((16, 80, 128), bf16), [VM, VM], 6, out_specs=VM, name="pack"
    )(index_query.reshape(16, 64, 128), index_weight.T)
    queries = exchanged(queries, "head")

    parts = wide_queries(at, jnp.transpose(query_latent, (1, 2, 0)), normalizer.T)
    query = [parts[0]]
    for part, d in zip(parts[1:], STEPS):
        query.append(along_x(part, d))
    part, index_keys = scores(query[:1], tiles)
    (part,) = scores(query[1:], tiles, part)
    sums = exchanged(part.reshape(4, 16, 2048), "head", ROW_ZH)

    prob = index_forward(at, kept, queries, index_keys, index_scale)
    own, send, dq = index_backward(at, kept, prob, queries, index_keys, sums, index_scale)

    got = other_core(send)
    dkey = (own + got.astype(f32)).astype(bf16)
    dkey = exchanged(dkey.reshape(32, 32, 128), ("seq", "head"), YZX)
    dkey = jnp.sum(dkey.astype(f32), axis=0).astype(bf16)
    dkey = jnp.broadcast_to(dkey, (16, 32, 128))
    both = exchanged(jnp.concatenate([dq, dkey], axis=1), "head")
    dq, dkey = call(
        last_body, (sds((16, 64, 128), bf16), sds((128, 128), f32)), [VM], 6, name="last"
    )(both)
    return dq.reshape(index_query.shape), dkey


def solution(mesh):
    return jax.shard_map(
        local,
        mesh=mesh,
        in_specs=(
            P("seq", "head", None),
            P("seq", None),
            P("seq", "head"),
            P("seq", "head", None),
            P("seq", None),
            P("seq", "head"),
            P("seq", None),
        ),
        out_specs=(P("seq", "head", None), P("seq", None)),
        check_vma=False,
    )
```
